32 devices in a mesh: bx: 8 (over y, x, core), by: 4 (over z).
Axes of the slice: x: 2, y: 2, z: 4, core: 2. Of those that a mesh axis runs over, the one named last changes fastest.
Arguments:
- interface_velocity: float32 [3, 2048, 2048], P(None, 'bx', 'by'), may hold values from -6 to 6
- history: float32 [6, 2, 3, 256, 8, 4, 512], P(None, None, None, 'by', 'bx'), may hold values from -6 to 6
- kernel: float32 [7, 256, 8, 4, 512], P(None, 'by', 'bx'), may hold values from -6 to 6
- velocity: float32 [3, 4, 2048, 2048], P(None, None, 'bx', 'by'), may hold values from -6 to 6
- stress: float32 [6, 4, 2048, 2048], P(None, None, 'bx', 'by'), may hold values from -6 to 6
- cohesion: float32 [4, 2048, 2048], P(None, 'bx', 'by'), may hold values from 0.5 to 4
Outputs:
- velocity_new: float32 [3, 4, 2048, 2048], P(None, None, 'bx', 'by')
- stress_new: float32 [6, 4, 2048, 2048], P(None, None, 'bx', 'by')
The draws below stay inside these ranges and needn't reach their ends.
All inputs are finite; a program needn't handle non-finite values.
Results may differ from the reference program's by a relative error of at most 0.00005.
Values sent between devices are 32-bit elements; how exact they have to be, the bound alone decides.
A program may use at most 192 MiB of HBM per device.

```python
import math
import jax
import jax.numpy as jnp
from jax import lax

NX = 2048
NY = 2048
NZ = 4
HIST = 6
CX = 256
CY = 512
STRIKE_PARTS = 8
DIP_PARTS = 4


def block_scale(key, dims, cuts, low, largest):
    level, own = 1.0, jax.random.fold_in(key, 6)
    for dim, shards_of in cuts:
        steps = jnp.exp(jax.random.uniform(jax.random.fold_in(own, dim), (shards_of,), jnp.float32, low / len(cuts), largest / len(cuts)))
        level = level * jnp.repeat(steps, dims[dim] // shards_of).reshape([-1 if axis == dim else 1 for axis in range(len(dims))])
    return level


def centred(key, shape, scale, bound, cuts=(), dtype=jnp.bfloat16):
    result = jax.random.normal(key, shape, jnp.float32) * scale
    if len(cuts) > 0:
        result = block_scale(key, shape, cuts, -0.22, 0.18) * result
    return jnp.clip(result, min=-bound, max=bound).astype(dtype)


def setup_inputs(seed: int = 0) -> dict:
    splits = jax.random.split(jax.random.key(seed), 7)
    return {
        "interface_velocity": centred(splits[0], (3, NX, NY), 1.0, 6.0, ((1, 8), (2, 4)), jnp.float32),
        "history": centred(splits[1], (HIST, 2, 3, CX, STRIKE_PARTS, DIP_PARTS, CY), 1.0, 6.0, ((3, 4), (4, 8)), jnp.float32),
        "kernel": centred(splits[2], (HIST + 1, CX, STRIKE_PARTS, DIP_PARTS, CY), ((HIST + 1) ** -0.5), 6.0, ((1, 4), (2, 8)), jnp.float32),
        "velocity": centred(splits[3], (3, NZ, NX, NY), 1.0, 6.0, ((2, 8), (3, 4)), jnp.float32),
        "stress": centred(splits[4], (6, NZ, NX, NY), 1.0, 6.0, ((2, 8), (3, 4)), jnp.float32),
        "cohesion": jnp.clip(jnp.exp(math.log(4.0) - 2.0794415 * jax.random.uniform(splits[5], (NZ, NX, NY), jnp.float32) ** block_scale(splits[5], (NZ, NX, NY), ((1, 8), (2, 4)), -0.2, 0.2)), 0.5, 4.0),
    }


COURANT = 0.3
FRICTION = 0.6

def to_layout(transform):
    stacked = jnp.stack([jnp.real(transform), jnp.imag(transform)])
    stacked = stacked.reshape(2, 3, CX, STRIKE_PARTS, CY, DIP_PARTS)
    return jnp.transpose(stacked, (0, 1, 2, 3, 5, 4))

def from_layout(stacked):
    ordered = jnp.transpose(stacked, (0, 1, 2, 3, 5, 4)).reshape(2, 3, NX, NY)
    return ordered[0] + 1j * ordered[1]

def strike_diff(padded):
    return 0.5 * (padded[..., 2:, 1:-1] - padded[..., :-2, 1:-1])

def dip_diff(padded):
    return 0.5 * (padded[..., 1:-1, 2:] - padded[..., 1:-1, :-2])

def depth_diff(layered, ghost_layer):
    above_layer = jnp.concatenate([layered[1:], jnp.zeros_like(layered[:1])], axis=0)
    below_layer = jnp.concatenate([ghost_layer[None], layered[:-1]], axis=0)
    return 0.5 * (above_layer - below_layer)

def yield_limit(trial_stress, cohesion):
    pressure = (trial_stress[0] + trial_stress[1] + trial_stress[2]) / 3.0
    normal_dev = trial_stress[:3] - pressure[None]
    second = 0.5 * lax.optimization_barrier(jnp.sum(normal_dev * normal_dev, axis=0)) + lax.optimization_barrier(jnp.sum(trial_stress[3:] * trial_stress[3:], axis=0))
    shear_stress = jnp.sqrt(second)
    yield_stress = cohesion + FRICTION * jnp.maximum(-pressure, 0.0)
    factor = yield_stress / jnp.maximum(shear_stress, yield_stress)
    return jnp.concatenate([pressure[None] + factor[None] * normal_dev, factor[None] * trial_stress[3:]], axis=0)

def advance_bulk(velocity, stress, traction, interface_velocity, cohesion, widen):
    padded_stress = widen(stress)
    forcing = jnp.stack([strike_diff(padded_stress[0]) + dip_diff(padded_stress[3]) + depth_diff(stress[4], traction[0]), strike_diff(padded_stress[3]) + dip_diff(padded_stress[1]) + depth_diff(stress[5], traction[1]), strike_diff(padded_stress[4]) + dip_diff(padded_stress[5]) + depth_diff(stress[2], traction[2])])
    velocity_new = velocity + COURANT * forcing
    padded_velocity = widen(velocity_new)
    strike_grad = strike_diff(padded_velocity)
    dip_grad = dip_diff(padded_velocity)
    depth_grad = jnp.stack([depth_diff(velocity_new[component], interface_velocity[component]) for component in range(3)])
    dilation = strike_grad[0] + dip_grad[1] + depth_grad[2]
    rates = jnp.stack([dilation + 2.0 * strike_grad[0], dilation + 2.0 * dip_grad[1], dilation + 2.0 * depth_grad[2], dip_grad[0] + strike_grad[1], depth_grad[0] + strike_grad[2], depth_grad[1] + dip_grad[2]])
    trial_stress = stress + COURANT * rates
    return (velocity_new, yield_limit(trial_stress, cohesion))

def wrap_pad(fields):
    return jnp.pad(fields, ((0, 0), (0, 0), (1, 1), (1, 1)), mode='wrap')

def reference(interface_velocity, history, kernel, velocity, stress, cohesion):
    transform = jnp.fft.fft2(interface_velocity, axes=(1, 2), norm='ortho')
    spectrum = to_layout(transform).astype(jnp.float32)
    past_terms = jnp.einsum('hupks,hzcupks->zcupks', kernel[1:].astype(jnp.float32), history.astype(jnp.float32), precision=lax.Precision.HIGHEST)
    response = kernel[0][None, None] * spectrum + past_terms
    traction = jnp.real(jnp.fft.ifft2(from_layout(response), axes=(1, 2), norm='ortho')).astype(jnp.float32)
    velocity_new, stress_new = advance_bulk(velocity, stress, traction, interface_velocity, cohesion, wrap_pad)
    return (velocity_new, stress_new)
```

```python
from functools import partial
import math

import jax
import jax.numpy as jnp
import numpy as np
from jax import lax
from jax.experimental import pallas as pl
from jax.experimental.pallas import tpu as pltpu
from jax.sharding import PartitionSpec as P

COURANT = 0.3
FRICTION = 0.6
F32 = jnp.float32
BF16 = jnp.bfloat16


def halves(table):
    high = np.asarray(table, np.float32).astype(BF16)
    low = (np.asarray(table, np.float64) - high.astype(np.float64)).astype(BF16)
    return np.stack([high, low])


def square_table(length):
    index = np.arange(length)
    angle = 2.0 * math.pi / length * (index[:, None] * index[None, :] % length)
    return jnp.asarray(np.stack([halves(np.cos(angle)), halves(np.sin(angle))]))


def split(value):
    high = value.astype(BF16)
    return high, (value - high.astype(F32)).astype(BF16)


def product(value, table, left):
    def dot(a, b):
        if left:
            a, b = b, a
        return lax.dot_general(a, b, (((1,), (0,)), ((), ())), preferred_element_type=F32)

    return dot(value[0], table[0]) + (dot(value[0], table[1]) + dot(value[1], table[0]))


def complex_product(real_part, imag_part, table_ref, sign, left):
    cos = (table_ref[0, 0], table_ref[0, 1])
    sin = (table_ref[1, 0], table_ref[1, 1])
    real_part, imag_part = split(real_part), split(imag_part)
    return (
        product(real_part, cos, left) - sign * product(imag_part, sin, left),
        product(imag_part, cos, left) + sign * product(real_part, sin, left),
    )


def root(index, count):
    angle = 2.0 * math.pi * (index % count) / count
    cos, sin = math.cos(angle), math.sin(angle)
    return [float(round(v)) if abs(v - round(v)) < 1e-12 else v for v in (cos, sin)]


def add_term(total, factor, value):
    if factor == 0.0:
        return total
    term = value if factor == 1.0 else (-value if factor == -1.0 else factor * value)
    return term if total is None else total + term


def strike_forward(count, x_ref, o_ref):
    for r in range(count):
        real_part = imag_part = None
        for b in range(count):
            cos, sin = root(r * b, count)
            real_part = add_term(real_part, cos, x_ref[b])
            imag_part = add_term(imag_part, -sin, x_ref[b])
        o_ref[r, 0] = real_part
        o_ref[r, 1] = jnp.zeros_like(real_part) if imag_part is None else imag_part


def strike_inverse(count, scale, x_ref, o_ref):
    for b in range(count):
        total = None
        for r in range(count):
            cos, sin = root(r * b, count)
            total = add_term(total, cos, x_ref[r, 0])
            total = add_term(total, -sin, x_ref[r, 1])
        o_ref[b] = scale * total


def strike_cells_dft(sign, x_ref, tw_ref, table_ref, o_ref, held):
    blocks, _, rows, _ = x_ref.shape
    for s in range(blocks):
        for z in range(2):
            held[z, pl.ds(s * rows, rows), :] = x_ref[s, z]
    cos, sin = tw_ref[:, 0:1], sign * tw_ref[:, 1:2]
    real_part, imag_part = held[0], held[1]
    if sign < 0:
        real_part, imag_part = (
            real_part * cos - imag_part * sin,
            real_part * sin + imag_part * cos,
        )
    real_part, imag_part = complex_product(real_part, imag_part, table_ref, sign, True)
    if sign > 0:
        real_part, imag_part = (
            real_part * cos - imag_part * sin,
            real_part * sin + imag_part * cos,
        )
    held[0] = real_part
    held[1] = imag_part
    blocks, _, rows, _ = o_ref.shape
    for s in range(blocks):
        for z in range(2):
            o_ref[s, z] = held[z, pl.ds(s * rows, rows), :]


def dip_forward(x_refs, tw_ref, table_ref, weight_ref, past_ref, held):
    count, _, rows, width = x_refs[0].shape
    for h, x_ref in enumerate(x_refs):
        part = slice(h * width, (h + 1) * width)
        for l in range(count):
            real_part = imag_part = None
            for j in range(count):
                cos, sin = root(l * j, count)
                real_part = add_term(real_part, cos, x_ref[j, 0])
                real_part = add_term(real_part, sin, x_ref[j, 1])
                imag_part = add_term(imag_part, cos, x_ref[j, 1])
                imag_part = add_term(imag_part, -sin, x_ref[j, 0])
            cos, sin = tw_ref[0, l : l + 1, part], tw_ref[1, l : l + 1, part]
            held[0, pl.ds(l * rows, rows), part] = real_part * cos + imag_part * sin
            held[1, pl.ds(l * rows, rows), part] = imag_part * cos - real_part * sin
    real_part, imag_part = complex_product(held[0], held[1], table_ref, -1.0, False)
    weight = weight_ref[...]
    held[0] = weight * real_part + past_ref[0]
    held[1] = weight * imag_part + past_ref[1]


def dip_inverse(held, tw_ref, table_ref, o_refs):
    count, _, rows, width = o_refs[0].shape
    real_part, imag_part = complex_product(held[0], held[1], table_ref, 1.0, False)
    held[0] = real_part
    held[1] = imag_part
    for l in range(count):
        cos, sin = tw_ref[0, l : l + 1, :], tw_ref[1, l : l + 1, :]
        real_part = held[0, pl.ds(l * rows, rows), :]
        imag_part = held[1, pl.ds(l * rows, rows), :]
        held[0, pl.ds(l * rows, rows), :] = real_part * cos - imag_part * sin
        held[1, pl.ds(l * rows, rows), :] = imag_part * cos + real_part * sin
    for h, o_ref in enumerate(o_refs):
        part = slice(h * width, (h + 1) * width)
        for j in range(count):
            real_part = imag_part = None
            for l in range(count):
                cos, sin = root(l * j, count)
                lr = held[0, pl.ds(l * rows, rows), part]
                li = held[1, pl.ds(l * rows, rows), part]
                real_part = add_term(real_part, cos, lr)
                real_part = add_term(real_part, -sin, li)
                imag_part = add_term(imag_part, cos, li)
                imag_part = add_term(imag_part, sin, lr)
            o_ref[j, 0] = real_part
            o_ref[j, 1] = imag_part


def rows_diff(value, before, after):
    count = value.shape[0]
    row = lax.broadcasted_iota(jnp.int32, value.shape, 0)
    low = jnp.where(row == 0, before, pltpu.roll(value, 1, 0))
    high = jnp.where(row == count - 1, after, pltpu.roll(value, count - 1, 0))
    return 0.5 * (high - low)


def cols_diff(value, before, after):
    count = value.shape[1]
    col = lax.broadcasted_iota(jnp.int32, value.shape, 1)
    low = jnp.where(col == 0, before, pltpu.roll(value, 1, 1))
    high = jnp.where(col == count - 1, after, pltpu.roll(value, count - 1, 1))
    return 0.5 * (high - low)


def stress_step(v_ref, prev_ref, next_ref, row_ref, col_ref, w_ref, s_ref, y_ref, n_ref, o_ref):
    layers = v_ref.shape[1]
    i, last = pl.program_id(0), pl.num_programs(0) - 1
    n_ref[...] = v_ref[...]
    for z in range(layers):
        dx, dy, dz = [], [], []
        for c in range(3):
            before = jnp.where(i == 0, row_ref[0, c, z, 7:8, :], prev_ref[c, z, 7:8, :])
            after = jnp.where(i == last, row_ref[1, c, z, 0:1, :], next_ref[c, z, 0:1, :])
            k = c * layers + z
            dx.append(rows_diff(v_ref[c, z], before, after))
            dy.append(
                cols_diff(v_ref[c, z], col_ref[0, :, k : k + 1], col_ref[1, :, k : k + 1])
            )
            low = w_ref[c] if z == 0 else v_ref[c, z - 1]
            if z + 1 < layers:
                dz.append(0.5 * (v_ref[c, z + 1] - low))
            else:
                dz.append(-0.5 * low)
        dilation = dx[0] + dy[1] + dz[2]
        xx = s_ref[0, z] + COURANT * (dilation + 2.0 * dx[0])
        yy = s_ref[1, z] + COURANT * (dilation + 2.0 * dy[1])
        zz = s_ref[2, z] + COURANT * (dilation + 2.0 * dz[2])
        xy = s_ref[3, z] + COURANT * (dy[0] + dx[1])
        xz = s_ref[4, z] + COURANT * (dz[0] + dx[2])
        yz = s_ref[5, z] + COURANT * (dz[1] + dy[2])
        pressure = (xx + yy + zz) / 3.0
        xx, yy, zz = xx - pressure, yy - pressure, zz - pressure
        shear = jnp.sqrt(0.5 * (xx * xx + yy * yy + zz * zz) + (xy * xy + xz * xz + yz * yz))
        limit = y_ref[z] + FRICTION * jnp.maximum(-pressure, 0.0)
        factor = limit / jnp.maximum(shear, limit)
        o_ref[0, z] = pressure + factor * xx
        o_ref[1, z] = pressure + factor * yy
        o_ref[2, z] = pressure + factor * zz
        o_ref[3, z] = factor * xy
        o_ref[4, z] = factor * xz
        o_ref[5, z] = factor * yz


def whole_block(shape):
    return pl.BlockSpec(shape, lambda *_: (0,) * len(shape))


def struct(shape):
    return jax.ShapeDtypeStruct(shape, F32)


def cost(flops, *arrays):
    moved = sum(math.prod(a.shape) * a.dtype.itemsize for a in arrays)
    return pl.CostEstimate(flops=int(flops), bytes_accessed=int(moved), transcendentals=0)


def fault_kernel(
    scale,
    face_ref,
    turns_ref,
    strike_table_ref,
    dip_tw_ref,
    dip_table_ref,
    kernel_ref,
    history_ref,
    velocity_ref,
    stress_ref,
    v_ref,
    row_ref,
    col_ref,
    x1,
    b1,
    b2,
    t1,
    t2,
    u1,
    u2,
    w2,
    held,
    held_part,
    weight,
    strike_tw_ref,
    lags,
    lag_held,
    past_ref,
    lag_sem,
    past_sem,
    send_sem,
    recv_sem,
    mirror_sem,
    o_ref,
    v_held,
    stress_held,
    edge_held,
    row_in,
    col_out,
    col_in,
    col_new,
    top_out,
    top_in,
    slab_sem,
    tile_sem,
    edge_sem,
    edge_recv,
):
    count, narrow = x1.shape[0], x1.shape[-1]
    w1, y1, now_ref = b1, x1, lags.at[0]
    parts = count // past_ref.shape[0]
    sizes = {"bx": lax.axis_size("bx"), "by": lax.axis_size("by")}
    place = {"bx": lax.axis_index("bx"), "by": lax.axis_index("by")}

    def device(axis, target):
        if axis == "bx":
            return (target, place["by"])
        return (place["bx"], target)

    strike, dip = place["bx"], place["by"]
    modes, zone = t2.shape[3], min(8, t2.shape[3])

    def active(target):
        return lax.rem(strike + target, 2) == 0

    full = active(dip)
    thin = jnp.logical_and(jnp.logical_not(full), strike == 0)
    forward = jnp.logical_or(full, strike == 0)
    mirror = (lax.rem(sizes["bx"] - strike, sizes["bx"]), sizes["by"] - 1 - dip)

    @pl.when(thin)
    def _():
        @pl.loop(0, count)
        def _(g):
            t2[g] = jnp.zeros(t2.shape[1:], F32)

    layers, cells, width = v_held.shape[1:]
    components = past_ref.shape[0]
    lag_loads = [
        pltpu.make_async_copy(
            kernel_ref.at[:, :, 0, l, :], lags.at[:, pl.ds(l * modes, modes), :], lag_sem.at[l]
        )
        for l in range(sizes["by"])
    ]

    def past_loads(i):
        slot = lax.rem(i, 2)
        return [
            pltpu.make_async_copy(
                history_ref.at[:, slot, lax.div(i, 2), :, 0, l, :],
                lag_held.at[slot, :, pl.ds(l * modes, modes), :],
                past_sem.at[slot, l],
            )
            for l in range(sizes["by"])
        ]

    for load in lag_loads:
        load.start()
    barrier = pltpu.get_barrier_semaphore()
    pl.semaphore_signal(barrier, 1, device_id=mirror, device_id_type=pl.DeviceIdType.MESH)
    for axis in ("bx", "by"):

        @pl.loop(1, sizes[axis])
        def _(k):
            target = lax.rem(place[axis] + k, sizes[axis])
            pl.semaphore_signal(
                barrier, 1, device_id=device(axis, target), device_id_type=pl.DeviceIdType.MESH
            )

    pl.semaphore_wait(barrier, sizes["bx"] + sizes["by"] - 1)

    swap = pltpu.make_async_remote_copy(
        src_ref=weight,
        dst_ref=weight,
        send_sem=mirror_sem.at[0],
        recv_sem=mirror_sem.at[1],
        device_id=mirror,
        device_id_type=pl.DeviceIdType.MESH,
    )


    def piece(ref, g, slot):
        if len(ref.shape) == 4 and ref.shape[0] != count:
            return ref.at[g // parts, slot, :, pl.ds(pl.multiple_of(g % parts * narrow, narrow), narrow)]
        if ref is face_ref or ref is o_ref:
            return ref.at[g, slot, :, pl.ds(0, narrow)]
        return ref.at[g, slot]

    def copy(stage, axis, c, k, source, landing):
        me = place[axis]
        target = lax.rem(me + k, sizes[axis])
        return pltpu.make_async_remote_copy(
            src_ref=piece(source, c, target),
            dst_ref=piece(landing, c, me),
            send_sem=send_sem.at[stage, c, k],
            recv_sem=recv_sem.at[stage, c, k],
            device_id=device(axis, target),
            device_id_type=pl.DeviceIdType.MESH,
        )

    def own(stage, axis, c, source, landing):
        me = place[axis]
        return pltpu.make_async_copy(
            piece(source, c, me), piece(landing, c, me), recv_sem.at[stage, c, 0]
        )

    def send(stage, axis, c, source, landing):
        @pl.loop(1, sizes[axis])
        def _(k):
            copy(stage, axis, c, k, source, landing).start()

        own(stage, axis, c, source, landing).start()

    def receive(stage, axis, c, source, landing):
        own(stage, axis, c, source, landing).wait()

        @pl.loop(1, sizes[axis])
        def _(k):
            copy(stage, axis, c, k, source, landing).wait()

    def tile(ref, g, slot):
        return ref.at[g, slot, :, pl.ds(0, zone), :]

    def lean(g, k):
        target = lax.rem(dip + k, sizes["by"])
        return pltpu.make_async_remote_copy(
            src_ref=tile(t1, g, target),
            dst_ref=tile(t2, g, dip),
            send_sem=send_sem.at[2, g, k],
            recv_sem=recv_sem.at[2, g, k],
            device_id=device("by", target),
            device_id_type=pl.DeviceIdType.MESH,
        )

    def lean_own(g):
        return pltpu.make_async_copy(tile(t1, g, dip), tile(t2, g, dip), recv_sem.at[2, g, 0])

    def each_forward(g, whole, part):
        @pl.loop(1, sizes["by"])
        def _(k):
            wanted = active(lax.rem(dip + k, sizes["by"]))

            @pl.when(wanted)
            def _():
                whole(copy(2, "by", g, k, t1, t2))

            @pl.when(jnp.logical_and(jnp.logical_not(wanted), strike == 0))
            def _():
                part(lean(g, k))

    def spread(g):
        each_forward(g, lambda c: c.start(), lambda c: c.start())

        @pl.when(full)
        def _():
            own(2, "by", g, t1, t2).start()

        @pl.when(thin)
        def _():
            lean_own(g).start()

    def spread_end(g):
        each_forward(g, lambda c: c.wait_send(), lambda c: c.wait_send())

    def gather(g):
        @pl.when(full)
        def _():
            own(2, "by", g, t1, t2).wait()

            @pl.loop(1, sizes["by"])
            def _(k):
                copy(2, "by", g, k, t1, t2).wait_recv()

        @pl.when(thin)
        def _():
            lean_own(g).wait()

            @pl.loop(1, sizes["by"])
            def _(k):
                lean(g, k).wait_recv()

    stages = (
        ("bx", face_ref, x1),
        ("bx", b1, b2),
        ("by", t1, t2),
        ("by", u1, u2),
        ("bx", w1, w2),
        ("bx", y1, o_ref),
    )

    def go(stage, g):
        axis, source, landing = stages[stage]
        send(stage, axis, g, source, landing)

    def take(stage, g):
        axis, source, landing = stages[stage]
        receive(stage, axis, g, source, landing)

    def enter(g):
        take(0, g)
        strike_forward(sizes["bx"], x1.at[g], b1.at[g])
        go(1, g)

    def across(g):
        take(1, g)
        strike_cells_dft(-1.0, b2.at[g], strike_tw_ref, strike_table_ref, t1.at[g], held_part)
        spread(g)

    def back(g):
        take(3, g)
        strike_cells_dft(1.0, u2.at[g], strike_tw_ref, strike_table_ref, w1.at[g], held_part)
        go(4, g)

    def leave(g):
        take(4, g)
        strike_inverse(sizes["bx"], scale, w2.at[g], y1.at[g])
        go(5, g)

    def remember(i):
        for load in past_loads(i):
            load.wait()
        slot = lax.rem(i, 2)

        @pl.loop(0, cells // 8)
        def _(k):
            rows = pl.ds(pl.multiple_of(k * 8, 8), 8)
            total = lags[1, rows, :] * lag_held[slot, 0, rows, :]
            for h in range(1, lag_held.shape[1]):
                total = total + lags[h + 1, rows, :] * lag_held[slot, h, rows, :]
            past_ref[lax.div(i, 2), slot, rows, :] = total

        @pl.when(i + 2 < 2 * components)
        def _():
            for load in past_loads(i + 2):
                load.start()

    def pick(rows, columns, total, wrap):
        at = lax.broadcasted_iota(jnp.int32, (rows, columns), 0)
        at = at + lax.broadcasted_iota(jnp.int32, (rows, columns), 1)
        at = jnp.where(at == total, 1.0, jnp.where(at == wrap, 1.0, 0.0))
        return at.astype(BF16)

    def place_all(value, table, left):
        total = None
        for _ in range(3):
            piece = value.astype(BF16)
            value = value - piece.astype(F32)
            a, b = (table, piece) if left else (piece, table)
            term = lax.dot_general(a, b, (((1,), (0,)), ((), ())), preferred_element_type=F32)
            total = term if total is None else total + term
        return total

    def mirrored():
        flip = pick(modes, modes, jnp.where(strike == 0, modes, modes - 1), -1)
        for l in range(sizes["by"]):
            other = (sizes["by"] - l) % sizes["by"]
            table = pick(width, width, width if l == 0 else width - 1, 0 if l == 0 else -1)
            value = place_all(now_ref[pl.ds(l * modes, modes), :], table, False)
            weight[pl.ds(other * modes, modes), :] = place_all(value, flip, True)

    def weigh():
        @pl.when(full)
        def _():
            swap.wait_recv()
            weight[...] = scale * (now_ref[...] + weight[...])

        @pl.when(thin)
        def _():
            swap.wait_send()
            row = lax.broadcasted_iota(jnp.int32, now_ref.shape, 0)
            weight[...] = jnp.where(lax.rem(row, modes) == 0, scale * now_ref[...], 0.0)

    def respond(c):
        @pl.when(forward)
        def _():
            for h in range(parts):
                gather(c * parts + h)
            dip_forward(
                [t2.at[c * parts + h] for h in range(parts)],
                dip_tw_ref,
                dip_table_ref,
                weight,
                past_ref.at[c],
                held,
            )

        @pl.when(jnp.logical_not(forward))
        def _():
            held[...] = past_ref[c]

        dip_inverse(
            held,
            dip_tw_ref,
            dip_table_ref,
            [u1.at[c * parts + h] for h in range(parts)],
        )
        for h in range(parts):
            go(3, c * parts + h)

    for load in past_loads(0) + past_loads(1):
        load.start()
    size = stress_held.shape[3] - 16
    tiles = cells // size
    block = col_out.shape[2]
    sources = ((0, 3, 4), (3, 1, 5), (4, 5, 2))
    up = {axis: lax.rem(place[axis] + 1, sizes[axis]) for axis in sizes}
    down = {axis: lax.rem(place[axis] + sizes[axis] - 1, sizes[axis]) for axis in sizes}

    def pair(axis, first, last, low, high, slot):
        return [
            pltpu.make_async_remote_copy(
                src_ref=source,
                dst_ref=landing,
                send_sem=edge_sem.at[slot + i],
                recv_sem=edge_recv.at[slot + i],
                device_id=device(axis, target[axis]),
                device_id_type=pl.DeviceIdType.MESH,
            )
            for i, (source, landing, target) in enumerate(((last, low, up), (first, high, down)))
        ]

    stress_rows = []
    for k, c in enumerate(sources[0]):
        stress_rows += pair(
            "bx",
            stress_ref.at[c, :, pl.ds(0, 8), :],
            stress_ref.at[c, :, pl.ds(cells - 8, 8), :],
            row_in.at[0, k],
            row_in.at[1, k],
            2 * k,
        )
    stress_cols = pair("by", col_out.at[0], col_out.at[1], col_in.at[0], col_in.at[1], 6)
    deep = pl.ds(1, layers - 1)
    deep_rows, top_rows = [
        pair(
            "bx",
            v_held.at[:, z, pl.ds(0, 8), :],
            v_held.at[:, z, pl.ds(cells - 8, 8), :],
            row_ref.at[0, :, z],
            row_ref.at[1, :, z],
            slot,
        )
        for z, slot in ((deep, 8), (0, 12))
    ]
    top_cols = pair("by", top_out.at[0], top_out.at[1], top_in.at[0], top_in.at[1], 14)
    new_cols = pair("by", col_new.at[0], col_new.at[1], col_ref.at[0], col_ref.at[1], 10)
    sides = (pl.ds(0, block), pl.ds(width - block, block))
    edge_loads = [
        pltpu.make_async_copy(
            stress_ref.at[c, :, :, side], edge_held.at[i, k], slab_sem.at[3 * i + k]
        )
        for i, side in enumerate(sides)
        for k, c in enumerate(sources[1])
    ]
    velocity_load = pltpu.make_async_copy(velocity_ref, v_held, slab_sem.at[6])
    deep_store = pltpu.make_async_copy(v_held.at[:, deep], v_ref.at[:, deep], slab_sem.at[7])
    top_store = pltpu.make_async_copy(v_held.at[:, 0], v_ref.at[:, 0], slab_sem.at[8])

    def tile_loads(t):
        slot = lax.rem(t, 2)
        row = pl.multiple_of(t * size, 8)
        before = pl.multiple_of(jnp.maximum(row - 8, 0), 8)
        after = pl.multiple_of(jnp.minimum(row + size, cells - 8), 8)
        loads = [
            pltpu.make_async_copy(
                stress_ref.at[:, :, pl.ds(row, size), :],
                stress_held.at[slot, :, :, pl.ds(8, size), :],
                tile_sem.at[slot, 0],
            )
        ]
        for k, c in enumerate(sources[0]):
            for i, (source, landing) in enumerate(((before, 0), (after, size + 8))):
                loads.append(
                    pltpu.make_async_copy(
                        stress_ref.at[c, :, pl.ds(source, 8), :],
                        stress_held.at[slot, c, :, pl.ds(landing, 8), :],
                        tile_sem.at[slot, 1 + 2 * k + i],
                    )
                )
        return loads

    def edges():
        for load in edge_loads:
            load.wait()
        for k in range(3):
            for z in range(layers):
                lane = pl.ds(k * layers + z, 1)
                col_out[0, :, lane] = edge_held[0, k, z, :, 0:1]
                col_out[1, :, lane] = edge_held[1, k, z, :, block - 1 : block]
        for c in stress_cols:
            c.start()

    def slab(t):
        @pl.when(t == 0)
        def _():
            velocity_load.wait()
            for c in stress_rows + stress_cols:
                c.wait_recv()

        @pl.when(t + 1 < tiles)
        def _():
            for load in tile_loads(t + 1):
                load.start()

        for load in tile_loads(t):
            load.wait()
        slot = lax.rem(t, 2)
        rows = pl.ds(pl.multiple_of(t * size, 8), size)
        for component, (sx, sy, sz) in enumerate(sources):
            for z in range(layers):
                k = component * layers + z
                before = jnp.where(t == 0, row_in[0, component, z, 7:8, :], stress_held[slot, sx, z, 7:8, :])
                after = jnp.where(
                    t == tiles - 1,
                    row_in[1, component, z, 0:1, :],
                    stress_held[slot, sx, z, size + 8 : size + 9, :],
                )
                total = rows_diff(stress_held[slot, sx, z, 8 : size + 8, :], before, after)
                total = total + cols_diff(
                    stress_held[slot, sy, z, 8 : size + 8, :],
                    col_in[0, rows, k : k + 1],
                    col_in[1, rows, k : k + 1],
                )
                if z + 1 < layers:
                    total = total + 0.5 * stress_held[slot, sz, z + 1, 8 : size + 8, :]
                if z > 0:
                    total = total - 0.5 * stress_held[slot, sz, z - 1, 8 : size + 8, :]
                value = v_held[component, z, rows, :] + COURANT * total
                v_held[component, z, rows, :] = value
                if z > 0:
                    col_new[0, rows, k : k + 1] = value[:, 0:1]
                    col_new[1, rows, k : k + 1] = value[:, width - 1 : width]

        @pl.when(t == tiles - 1)
        def _():
            deep_store.start()
            for c in deep_rows + new_cols:
                c.start()

    go(0, 0)
    go(0, 1)
    for load in edge_loads:
        load.start()
    for c in stress_rows:
        c.start()
    velocity_load.start()
    for load in tile_loads(0):
        load.start()
    turns = turns_ref[strike]
    strike_tw_ref[...] = jnp.concatenate([turns, jnp.zeros((block - 8, cells), F32)], axis=0).T
    for load in lag_loads:
        load.wait()
    first_tile = 3
    first_back = count + 1
    gap = first_back + parts

    def turn_of(s):
        last, none = components - 1, components
        whole = lax.rem(s + parts - 1, parts) == 0
        step = lax.div(s - 1, parts)
        now = jnp.where(jnp.logical_and(whole, step >= 2), step - 2, none)
        now = jnp.where(now >= last, none, now)
        now = jnp.where(s == gap + 1, last, now)
        early = jnp.where(jnp.logical_and(whole, s > 0), step, none)
        early = jnp.where(jnp.logical_or(s == 0, early >= last), none, early)
        early = jnp.where(s == 0, 0, jnp.where(early == 0, none, early))
        early = jnp.where(s == first_back + 1, last, early)
        return jnp.where(forward, now, early)

    @pl.loop(0, first_back + count + 2)
    def _(s):
        @pl.when(jnp.logical_and(forward, s == 2 * parts + 1))
        def _():
            weigh()

        @pl.when(s < components)
        def _():
            remember(2 * s)
            remember(2 * s + 1)

        turn = turn_of(s)

        @pl.when(turn < components)
        def _():
            respond(turn)

        @pl.when(s < count)
        def _():
            enter(s)

        @pl.when(s + 2 < count)
        def _():
            go(0, s + 2)

        @pl.when(jnp.logical_and(s > 0, s <= count))
        def _():
            across(s - 1)

        @pl.when(s == 0)
        def _():
            edges()

        @pl.when(jnp.logical_and(s == 1, jnp.logical_not(full)))
        def _():
            mirrored()
            swap.start()

        turned = s - first_back - (s > gap).astype(jnp.int32)

        @pl.when(jnp.logical_and(jnp.logical_and(turned >= 0, turned < count), s != gap))
        def _():
            back(turned)

        done = s - first_back - 1 - (s > gap + 1).astype(jnp.int32)

        @pl.when(jnp.logical_and(jnp.logical_and(done >= 0, done < count), s != gap + 1))
        def _():
            leave(done)

        @pl.when(jnp.logical_and(s >= first_tile, s < tiles + first_tile))
        def _():
            slab(s - first_tile)

    @pl.when(jnp.logical_not(forward))
    def _():
        swap.wait_send()

    @pl.loop(0, count)
    def _(g):
        take(5, g)
        spread_end(g)
        c = lax.div(g, parts)
        lanes = pl.ds(pl.multiple_of(lax.rem(g, parts) * narrow, narrow), narrow)
        high = cells // sizes["bx"]
        for b in range(sizes["bx"]):
            rows = pl.ds(b * high, high)
            v_held[c, 0, rows, lanes] = v_held[c, 0, rows, lanes] - (0.5 * COURANT) * o_ref[c, b, :, lanes]

    for c in top_rows:
        c.start()
    top_store.start()
    lane = lax.broadcasted_iota(jnp.int32, (cells, block), 1)
    for i, side in enumerate((0, width - block)):
        at = block - 1 if i else 0
        total = jnp.zeros((cells, block), F32)
        for c in range(components):
            value = v_held[c, 0, :, side : side + block][:, at : at + 1]
            total = jnp.where(lane == c, value, total)
        top_out[i] = total.T[:8]
    for c in top_cols:
        c.start()
    for c in new_cols + deep_rows + top_cols:
        c.wait_recv()
    for i in range(2):
        filled = jnp.concatenate([top_in[i], jnp.zeros((block - 8, cells), F32)], axis=0).T
        for c in range(components):
            col_ref[i, :, c * layers : c * layers + 1] = filled[:, c : c + 1]
    deep_store.wait()
    top_store.wait()
    for c in stress_rows + stress_cols + new_cols + deep_rows + top_cols:
        c.wait_send()
    for c in top_rows:
        c.wait()


def fault_velocity(interface, kernel, history, tables, velocity, stress, scale):
    strike_count, dip_count = lax.axis_size("bx"), lax.axis_size("by")
    count, cells, width = interface.shape
    rows, modes = cells // strike_count, cells // dip_count
    parts = 2 if width % 256 == 0 else 1
    narrow = width // parts
    face = interface.reshape(count, strike_count, rows, width)
    chunks = count * parts
    flat = (chunks, strike_count, rows, narrow)
    wide = (chunks, strike_count, 2, rows, narrow)
    tall = (chunks, dip_count, 2, modes, narrow)
    peers = max(strike_count, dip_count)
    layers = velocity.shape[1]
    tile, block = min(32, cells), min(128, width)
    operands = (face, *tables, kernel, history, velocity, stress)
    vmem, anywhere = pl.BlockSpec(memory_space=pltpu.VMEM), pl.BlockSpec(memory_space=pl.ANY)
    return pl.pallas_call(
        partial(fault_kernel, scale),
        out_shape=[
            struct(velocity.shape),
            struct((2, count, layers, 8, width)),
            struct((2, cells, block)),
        ],
        in_specs=[anywhere] + [vmem] * len(tables) + [anywhere] * 4,
        out_specs=[anywhere, vmem, vmem],
        scratch_shapes=[
            *[pltpu.VMEM(s, F32) for s in (flat, wide, wide, tall, tall, tall, tall, wide)],
            pltpu.VMEM((2, cells, width), F32),
            pltpu.VMEM((2, cells, narrow), F32),
            pltpu.VMEM((cells, width), F32),
            pltpu.VMEM((cells, block), F32),
            pltpu.VMEM((kernel.shape[0], cells, width), F32),
            pltpu.VMEM((2, history.shape[0], cells, width), F32),
            pltpu.VMEM((count, 2, cells, width), F32),
            pltpu.SemaphoreType.DMA((dip_count,)),
            pltpu.SemaphoreType.DMA((2, dip_count)),
            pltpu.SemaphoreType.DMA((6, chunks, peers)),
            pltpu.SemaphoreType.DMA((6, chunks, peers)),
            pltpu.SemaphoreType.DMA((2,)),
            pltpu.VMEM(face.shape, F32),
            pltpu.VMEM(velocity.shape, F32),
            pltpu.VMEM((2, 6, layers, tile + 16, width), F32),
            pltpu.VMEM((2, 3, layers, cells, block), F32),
            pltpu.VMEM((2, 3, layers, 8, width), F32),
            pltpu.VMEM((2, cells, block), F32),
            pltpu.VMEM((2, cells, block), F32),
            pltpu.VMEM((2, cells, block), F32),
            pltpu.VMEM((2, 8, cells), F32),
            pltpu.VMEM((2, 8, cells), F32),
            pltpu.SemaphoreType.DMA((9,)),
            pltpu.SemaphoreType.DMA((2, 7)),
            pltpu.SemaphoreType.DMA((16,)),
            pltpu.SemaphoreType.DMA((16,)),
        ],
        compiler_params=pltpu.CompilerParams(
            collective_id=0, has_side_effects=True, vmem_limit_bytes=63 * 1024 * 1024
        ),
        name="fault_velocity",
    )(*operands)


def tile_spec(shape, tile):
    block = shape[:-2] + (tile, shape[-1])
    lead = (0,) * (len(shape) - 2)
    return pl.BlockSpec(block, lambda i: lead + (i, 0))


def halo_specs(shape, tile):
    block = shape[:-2] + (8, shape[-1])
    lead = (0,) * (len(shape) - 2)
    step, last = tile // 8, shape[-2] // 8 - 1
    return [
        pl.BlockSpec(block, lambda i: lead + (jnp.maximum(i * step - 1, 0), 0)),
        pl.BlockSpec(block, lambda i: lead + (jnp.minimum((i + 1) * step, last), 0)),
    ]


def local(interface_velocity, history, kernel, velocity, stress, cohesion):
    strike_count, dip_count = lax.axis_size("bx"), lax.axis_size("by")
    _, layers, cells, width = velocity.shape
    strike_length, dip_length = cells * strike_count, width * dip_count
    scale = 1.0 / math.sqrt(strike_length * dip_length)
    turn = np.outer(np.arange(strike_count), np.arange(cells)) * (2.0 * math.pi / strike_length)
    turns = np.zeros((strike_count, 8, cells), np.float32)
    turns[:, 0], turns[:, 1] = np.cos(turn), np.sin(turn)
    lane = np.outer(np.arange(dip_count), np.arange(width)) * (2.0 * math.pi / dip_length)
    dip_tw = jnp.asarray(np.stack([np.cos(lane), np.sin(lane)]).astype(np.float32))
    dip_table = square_table(width)
    strike_table = square_table(cells)
    tables = (jnp.asarray(turns), strike_table, dip_tw, dip_table)

    velocity_part, rows, cols = fault_velocity(
        interface_velocity, kernel, history, tables, velocity, stress, scale
    )
    tile = min(64, cells)
    return pl.pallas_call(
        stress_step,
        grid=(cells // tile,),
        in_specs=[
            tile_spec(velocity.shape, tile),
            *halo_specs(velocity.shape, tile),
            whole_block(rows.shape),
            tile_spec(cols.shape, tile),
            tile_spec(interface_velocity.shape, tile),
            tile_spec(stress.shape, tile),
            tile_spec(cohesion.shape, tile),
        ],
        out_specs=[tile_spec(velocity.shape, tile), tile_spec(stress.shape, tile)],
        out_shape=[struct(velocity.shape), struct(stress.shape)],
        cost_estimate=cost(2e7, stress, stress, velocity),
        name="stress_step",
    )(velocity_part, velocity_part, velocity_part, rows, cols, interface_velocity, stress, cohesion)


def solution(mesh):
    return jax.shard_map(
        local,
        mesh=mesh,
        in_specs=(
            P(None, "bx", "by"),
            P(None, None, None, "by", "bx", None, None),
            P(None, "by", "bx", None, None),
            P(None, None, "bx", "by"),
            P(None, None, "bx", "by"),
            P(None, "bx", "by"),
        ),
        out_specs=(P(None, None, "bx", "by"), P(None, None, "bx", "by")),
        check_vma=False,
    )
```

```python
from functools import partial
import math

import jax
import jax.numpy as jnp
import numpy as np
from jax import lax
from jax.experimental import pallas as pl
from jax.experimental.pallas import tpu as pltpu
from jax.sharding import PartitionSpec as P

COURANT = 0.3
FRICTION = 0.6
F32 = jnp.float32
BF16 = jnp.bfloat16


def halves(table):
    high = np.asarray(table, np.float32).astype(BF16)
    low = (np.asarray(table, np.float64) - high.astype(np.float64)).astype(BF16)
    return np.stack([high, low])


def square_table(length):
    index = np.arange(length)
    angle = 2.0 * math.pi / length * (index[:, None] * index[None, :] % length)
    return jnp.asarray(np.stack([halves(np.cos(angle)), halves(np.sin(angle))]))


def split(value):
    high = value.astype(BF16)
    return high, (value - high.astype(F32)).astype(BF16)


def product(value, table, left):
    def dot(a, b):
        if left:
            a, b = b, a
        return lax.dot_general(a, b, (((1,), (0,)), ((), ())), preferred_element_type=F32)

    return dot(value[0], table[0]) + (dot(value[0], table[1]) + dot(value[1], table[0]))


def complex_product(real_part, imag_part, table_ref, sign, left):
    cos = (table_ref[0, 0], table_ref[0, 1])
    sin = (table_ref[1, 0], table_ref[1, 1])
    real_part, imag_part = split(real_part), split(imag_part)
    return (
        product(real_part, cos, left) - sign * product(imag_part, sin, left),
        product(imag_part, cos, left) + sign * product(real_part, sin, left),
    )


def root(index, count):
    angle = 2.0 * math.pi * (index % count) / count
    cos, sin = math.cos(angle), math.sin(angle)
    return [float(round(v)) if abs(v - round(v)) < 1e-12 else v for v in (cos, sin)]


def add_term(total, factor, value):
    if factor == 0.0:
        return total
    term = value if factor == 1.0 else (-value if factor == -1.0 else factor * value)
    return term if total is None else total + term


def strike_forward(count, x_ref, o_ref):
    for r in range(count):
        real_part = imag_part = None
        for b in range(count):
            cos, sin = root(r * b, count)
            real_part = add_term(real_part, cos, x_ref[b])
            imag_part = add_term(imag_part, -sin, x_ref[b])
        o_ref[r, 0] = real_part
        o_ref[r, 1] = jnp.zeros_like(real_part) if imag_part is None else imag_part


def strike_inverse(count, scale, x_ref, o_ref):
    for b in range(count):
        total = None
        for r in range(count):
            cos, sin = root(r * b, count)
            total = add_term(total, cos, x_ref[r, 0])
            total = add_term(total, -sin, x_ref[r, 1])
        o_ref[b] = scale * total


def strike_cells_dft(sign, x_ref, tw_ref, table_ref, o_ref, held):
    blocks, _, rows, _ = x_ref.shape
    for s in range(blocks):
        for z in range(2):
            held[z, pl.ds(s * rows, rows), :] = x_ref[s, z]
    cos, sin = tw_ref[:, 0:1], sign * tw_ref[:, 1:2]
    real_part, imag_part = held[0], held[1]
    if sign < 0:
        real_part, imag_part = (
            real_part * cos - imag_part * sin,
            real_part * sin + imag_part * cos,
        )
    real_part, imag_part = complex_product(real_part, imag_part, table_ref, sign, True)
    if sign > 0:
        real_part, imag_part = (
            real_part * cos - imag_part * sin,
            real_part * sin + imag_part * cos,
        )
    held[0] = real_part
    held[1] = imag_part
    blocks, _, rows, _ = o_ref.shape
    for s in range(blocks):
        for z in range(2):
            o_ref[s, z] = held[z, pl.ds(s * rows, rows), :]


def dip_forward(x_refs, tw_ref, table_ref, weight_ref, past_ref, held):
    count, _, rows, width = x_refs[0].shape
    for h, x_ref in enumerate(x_refs):
        part = slice(h * width, (h + 1) * width)
        for l in range(count):
            real_part = imag_part = None
            for j in range(count):
                cos, sin = root(l * j, count)
                real_part = add_term(real_part, cos, x_ref[j, 0])
                real_part = add_term(real_part, sin, x_ref[j, 1])
                imag_part = add_term(imag_part, cos, x_ref[j, 1])
                imag_part = add_term(imag_part, -sin, x_ref[j, 0])
            cos, sin = tw_ref[0, l : l + 1, part], tw_ref[1, l : l + 1, part]
            held[0, pl.ds(l * rows, rows), part] = real_part * cos + imag_part * sin
            held[1, pl.ds(l * rows, rows), part] = imag_part * cos - real_part * sin
    real_part, imag_part = complex_product(held[0], held[1], table_ref, -1.0, False)
    weight = weight_ref[...]
    held[0] = weight * real_part + past_ref[0]
    held[1] = weight * imag_part + past_ref[1]


def dip_inverse(held, tw_ref, table_ref, o_refs):
    count, _, rows, width = o_refs[0].shape
    real_part, imag_part = complex_product(held[0], held[1], table_ref, 1.0, False)
    held[0] = real_part
    held[1] = imag_part
    for l in range(count):
        cos, sin = tw_ref[0, l : l + 1, :], tw_ref[1, l : l + 1, :]
        real_part = held[0, pl.ds(l * rows, rows), :]
        imag_part = held[1, pl.ds(l * rows, rows), :]
        held[0, pl.ds(l * rows, rows), :] = real_part * cos - imag_part * sin
        held[1, pl.ds(l * rows, rows), :] = imag_part * cos + real_part * sin
    for h, o_ref in enumerate(o_refs):
        part = slice(h * width, (h + 1) * width)
        for j in range(count):
            real_part = imag_part = None
            for l in range(count):
                cos, sin = root(l * j, count)
                lr = held[0, pl.ds(l * rows, rows), part]
                li = held[1, pl.ds(l * rows, rows), part]
                real_part = add_term(real_part, cos, lr)
                real_part = add_term(real_part, -sin, li)
                imag_part = add_term(imag_part, cos, li)
                imag_part = add_term(imag_part, sin, lr)
            o_ref[j, 0] = real_part
            o_ref[j, 1] = imag_part


def rows_diff(value, before, after):
    count = value.shape[0]
    row = lax.broadcasted_iota(jnp.int32, value.shape, 0)
    low = jnp.where(row == 0, before, pltpu.roll(value, 1, 0))
    high = jnp.where(row == count - 1, after, pltpu.roll(value, count - 1, 0))
    return 0.5 * (high - low)


def cols_diff(value, before, after):
    count = value.shape[1]
    col = lax.broadcasted_iota(jnp.int32, value.shape, 1)
    low = jnp.where(col == 0, before, pltpu.roll(value, 1, 1))
    high = jnp.where(col == count - 1, after, pltpu.roll(value, count - 1, 1))
    return 0.5 * (high - low)


def stress_step(v_ref, prev_ref, next_ref, row_ref, col_ref, w_ref, s_ref, y_ref, n_ref, o_ref):
    layers = v_ref.shape[1]
    i, last = pl.program_id(0), pl.num_programs(0) - 1
    n_ref[...] = v_ref[...]
    for z in range(layers):
        dx, dy, dz = [], [], []
        for c in range(3):
            before = jnp.where(i == 0, row_ref[0, c, z, 7:8, :], prev_ref[c, z, 7:8, :])
            after = jnp.where(i == last, row_ref[1, c, z, 0:1, :], next_ref[c, z, 0:1, :])
            k = c * layers + z
            dx.append(rows_diff(v_ref[c, z], before, after))
            dy.append(
                cols_diff(v_ref[c, z], col_ref[0, :, k : k + 1], col_ref[1, :, k : k + 1])
            )
            low = w_ref[c] if z == 0 else v_ref[c, z - 1]
            if z + 1 < layers:
                dz.append(0.5 * (v_ref[c, z + 1] - low))
            else:
                dz.append(-0.5 * low)
        dilation = dx[0] + dy[1] + dz[2]
        xx = s_ref[0, z] + COURANT * (dilation + 2.0 * dx[0])
        yy = s_ref[1, z] + COURANT * (dilation + 2.0 * dy[1])
        zz = s_ref[2, z] + COURANT * (dilation + 2.0 * dz[2])
        xy = s_ref[3, z] + COURANT * (dy[0] + dx[1])
        xz = s_ref[4, z] + COURANT * (dz[0] + dx[2])
        yz = s_ref[5, z] + COURANT * (dz[1] + dy[2])
        pressure = (xx + yy + zz) / 3.0
        xx, yy, zz = xx - pressure, yy - pressure, zz - pressure
        shear = jnp.sqrt(0.5 * (xx * xx + yy * yy + zz * zz) + (xy * xy + xz * xz + yz * yz))
        limit = y_ref[z] + FRICTION * jnp.maximum(-pressure, 0.0)
        factor = limit / jnp.maximum(shear, limit)
        o_ref[0, z] = pressure + factor * xx
        o_ref[1, z] = pressure + factor * yy
        o_ref[2, z] = pressure + factor * zz
        o_ref[3, z] = factor * xy
        o_ref[4, z] = factor * xz
        o_ref[5, z] = factor * yz


def whole_block(shape):
    return pl.BlockSpec(shape, lambda *_: (0,) * len(shape))


def struct(shape):
    return jax.ShapeDtypeStruct(shape, F32)


def cost(flops, *arrays):
    moved = sum(math.prod(a.shape) * a.dtype.itemsize for a in arrays)
    return pl.CostEstimate(flops=int(flops), bytes_accessed=int(moved), transcendentals=0)


def fault_kernel(
    scale,
    face_ref,
    turns_ref,
    strike_table_ref,
    dip_tw_ref,
    dip_table_ref,
    kernel_ref,
    history_ref,
    velocity_ref,
    stress_ref,
    v_ref,
    row_ref,
    col_ref,
    x1,
    b1,
    b2,
    t1,
    t2,
    u1,
    u2,
    w2,
    held,
    held_part,
    weight,
    strike_tw_ref,
    lags,
    lag_held,
    past_ref,
    lag_sem,
    past_sem,
    send_sem,
    recv_sem,
    mirror_sem,
    o_ref,
    v_held,
    stress_held,
    edge_held,
    row_in,
    col_out,
    col_in,
    col_new,
    top_out,
    top_in,
    slab_sem,
    tile_sem,
    edge_sem,
    edge_recv,
):
    count, narrow = x1.shape[0], x1.shape[-1]
    w1, y1, now_ref = b1, x1, lags.at[0]
    parts = count // past_ref.shape[0]
    sizes = {"bx": lax.axis_size("bx"), "by": lax.axis_size("by")}
    place = {"bx": lax.axis_index("bx"), "by": lax.axis_index("by")}

    def device(axis, target):
        if axis == "bx":
            return (target, place["by"])
        return (place["bx"], target)

    strike, dip = place["bx"], place["by"]
    modes, zone = t2.shape[3], min(8, t2.shape[3])

    def active(target):
        return lax.rem(strike + target, 2) == 0

    full = active(dip)
    thin = jnp.logical_and(jnp.logical_not(full), strike == 0)
    forward = jnp.logical_or(full, strike == 0)
    mirror = (lax.rem(sizes["bx"] - strike, sizes["bx"]), sizes["by"] - 1 - dip)

    @pl.when(thin)
    def _():
        @pl.loop(0, count)
        def _(g):
            t2[g] = jnp.zeros(t2.shape[1:], F32)

    layers, cells, width = v_held.shape[1:]
    components = past_ref.shape[0]
    lag_loads = [
        pltpu.make_async_copy(
            kernel_ref.at[:, :, 0, l, :], lags.at[:, pl.ds(l * modes, modes), :], lag_sem.at[l]
        )
        for l in range(sizes["by"])
    ]

    def past_loads(i):
        slot = lax.rem(i, 2)
        return [
            pltpu.make_async_copy(
                history_ref.at[:, slot, lax.div(i, 2), :, 0, l, :],
                lag_held.at[slot, :, pl.ds(l * modes, modes), :],
                past_sem.at[slot, l],
            )
            for l in range(sizes["by"])
        ]

    for load in lag_loads:
        load.start()
    barrier = pltpu.get_barrier_semaphore()
    pl.semaphore_signal(barrier, 1, device_id=mirror, device_id_type=pl.DeviceIdType.MESH)
    for axis in ("bx", "by"):

        @pl.loop(1, sizes[axis])
        def _(k):
            target = lax.rem(place[axis] + k, sizes[axis])
            pl.semaphore_signal(
                barrier, 1, device_id=device(axis, target), device_id_type=pl.DeviceIdType.MESH
            )

    pl.semaphore_wait(barrier, sizes["bx"] + sizes["by"] - 1)

    swap = pltpu.make_async_remote_copy(
        src_ref=weight,
        dst_ref=weight,
        send_sem=mirror_sem.at[0],
        recv_sem=mirror_sem.at[1],
        device_id=mirror,
        device_id_type=pl.DeviceIdType.MESH,
    )


    def piece(ref, g, slot):
        if len(ref.shape) == 4 and ref.shape[0] != count:
            return ref.at[g // parts, slot, :, pl.ds(pl.multiple_of(g % parts * narrow, narrow), narrow)]
        if ref is face_ref or ref is o_ref:
            return ref.at[g, slot, :, pl.ds(0, narrow)]
        return ref.at[g, slot]

    def several(ref, g, number):
        if len(ref.shape) == 4 and ref.shape[0] != count:
            lanes = pl.ds(pl.multiple_of(g % parts * narrow, narrow), narrow)
            return ref.at[g // parts, pl.ds(0, number), :, lanes]
        return ref.at[g, pl.ds(0, number)]

    def settle(ref, sem):
        pltpu.make_async_copy(ref, ref, sem).wait()

    def copy(stage, axis, c, k, source, landing):
        me = place[axis]
        target = lax.rem(me + k, sizes[axis])
        return pltpu.make_async_remote_copy(
            src_ref=piece(source, c, target),
            dst_ref=piece(landing, c, me),
            send_sem=send_sem.at[stage, c],
            recv_sem=recv_sem.at[stage, c],
            device_id=device(axis, target),
            device_id_type=pl.DeviceIdType.MESH,
        )

    def own(stage, axis, c, source, landing):
        me = place[axis]
        return pltpu.make_async_copy(
            piece(source, c, me), piece(landing, c, me), recv_sem.at[stage, c]
        )

    def send(stage, axis, c, source, landing):
        @pl.loop(1, sizes[axis])
        def _(k):
            copy(stage, axis, c, k, source, landing).start()

        own(stage, axis, c, source, landing).start()

    def receive(stage, axis, c, source, landing):
        settle(several(landing, c, sizes[axis]), recv_sem.at[stage, c])
        settle(several(landing, c, sizes[axis] - 1), send_sem.at[stage, c])

    def tile(ref, g, slot):
        return ref.at[g, slot, :, pl.ds(0, zone), :]

    def lean(g, k):
        target = lax.rem(dip + k, sizes["by"])
        return pltpu.make_async_remote_copy(
            src_ref=tile(t1, g, target),
            dst_ref=tile(t2, g, dip),
            send_sem=send_sem.at[6, g],
            recv_sem=recv_sem.at[2, g],
            device_id=device("by", target),
            device_id_type=pl.DeviceIdType.MESH,
        )

    def lean_own(g):
        return pltpu.make_async_copy(tile(t1, g, dip), tile(t2, g, dip), recv_sem.at[2, g])

    def spread(g):
        @pl.loop(1, sizes["by"])
        def _(k):
            wanted = active(lax.rem(dip + k, sizes["by"]))

            @pl.when(wanted)
            def _():
                copy(2, "by", g, k, t1, t2).start()

            @pl.when(jnp.logical_and(jnp.logical_not(wanted), strike == 0))
            def _():
                lean(g, k).start()

        @pl.when(full)
        def _():
            own(2, "by", g, t1, t2).start()

        @pl.when(thin)
        def _():
            lean_own(g).start()

    half = sizes["by"] // 2

    def spread_end(g):
        def wait(condition, number, zoned):
            @pl.when(condition)
            def _():
                if zoned:
                    settle(t1.at[g, pl.ds(0, number), :, pl.ds(0, zone), :], send_sem.at[6, g])
                else:
                    settle(t1.at[g, pl.ds(0, number)], send_sem.at[2, g])

        wait(full, half - 1, False)
        wait(jnp.logical_not(full), half, False)
        wait(jnp.logical_and(full, strike == 0), half, True)
        wait(thin, half - 1, True)

    def gather(g):
        @pl.when(full)
        def _():
            settle(t2.at[g], recv_sem.at[2, g])

        @pl.when(thin)
        def _():
            settle(t2.at[g, :, :, pl.ds(0, zone), :], recv_sem.at[2, g])

    stages = (
        ("bx", face_ref, x1),
        ("bx", b1, b2),
        ("by", t1, t2),
        ("by", u1, u2),
        ("bx", w1, w2),
        ("bx", y1, o_ref),
    )

    def go(stage, g):
        axis, source, landing = stages[stage]
        send(stage, axis, g, source, landing)

    def take(stage, g):
        axis, source, landing = stages[stage]
        receive(stage, axis, g, source, landing)

    def enter(g):
        take(0, g)
        strike_forward(sizes["bx"], x1.at[g], b1.at[g])
        go(1, g)

    def across(g):
        take(1, g)
        strike_cells_dft(-1.0, b2.at[g], strike_tw_ref, strike_table_ref, t1.at[g], held_part)
        spread(g)

    def back(g):
        take(3, g)
        strike_cells_dft(1.0, u2.at[g], strike_tw_ref, strike_table_ref, w1.at[g], held_part)
        go(4, g)

    def leave(g):
        take(4, g)
        strike_inverse(sizes["bx"], scale, w2.at[g], y1.at[g])
        go(5, g)

    def remember(i):
        for load in past_loads(i):
            load.wait()
        slot = lax.rem(i, 2)

        @pl.loop(0, cells // 8)
        def _(k):
            rows = pl.ds(pl.multiple_of(k * 8, 8), 8)
            total = lags[1, rows, :] * lag_held[slot, 0, rows, :]
            for h in range(1, lag_held.shape[1]):
                total = total + lags[h + 1, rows, :] * lag_held[slot, h, rows, :]
            past_ref[lax.div(i, 2), slot, rows, :] = total

        @pl.when(i + 2 < 2 * components)
        def _():
            for load in past_loads(i + 2):
                load.start()

    def pick(rows, columns, total, wrap):
        at = lax.broadcasted_iota(jnp.int32, (rows, columns), 0)
        at = at + lax.broadcasted_iota(jnp.int32, (rows, columns), 1)
        at = jnp.where(at == total, 1.0, jnp.where(at == wrap, 1.0, 0.0))
        return at.astype(BF16)

    def place_all(value, table, left):
        total = None
        for _ in range(3):
            piece = value.astype(BF16)
            value = value - piece.astype(F32)
            a, b = (table, piece) if left else (piece, table)
            term = lax.dot_general(a, b, (((1,), (0,)), ((), ())), preferred_element_type=F32)
            total = term if total is None else total + term
        return total

    def mirrored():
        flip = pick(modes, modes, jnp.where(strike == 0, modes, modes - 1), -1)
        for l in range(sizes["by"]):
            other = (sizes["by"] - l) % sizes["by"]
            table = pick(width, width, width if l == 0 else width - 1, 0 if l == 0 else -1)
            value = place_all(now_ref[pl.ds(l * modes, modes), :], table, False)
            weight[pl.ds(other * modes, modes), :] = place_all(value, flip, True)

    def weigh():
        @pl.when(full)
        def _():
            swap.wait_recv()
            weight[...] = scale * (now_ref[...] + weight[...])

        @pl.when(thin)
        def _():
            swap.wait_send()
            row = lax.broadcasted_iota(jnp.int32, now_ref.shape, 0)
            weight[...] = jnp.where(lax.rem(row, modes) == 0, scale * now_ref[...], 0.0)

    def respond(c):
        @pl.when(forward)
        def _():
            for h in range(parts):
                gather(c * parts + h)
            dip_forward(
                [t2.at[c * parts + h] for h in range(parts)],
                dip_tw_ref,
                dip_table_ref,
                weight,
                past_ref.at[c],
                held,
            )

        @pl.when(jnp.logical_not(forward))
        def _():
            held[...] = past_ref[c]

        dip_inverse(
            held,
            dip_tw_ref,
            dip_table_ref,
            [u1.at[c * parts + h] for h in range(parts)],
        )
        for h in range(parts):
            go(3, c * parts + h)

    for load in past_loads(0) + past_loads(1):
        load.start()
    size = stress_held.shape[3] - 16
    tiles = cells // size
    block = col_out.shape[2]
    sources = ((0, 3, 4), (3, 1, 5), (4, 5, 2))
    up = {axis: lax.rem(place[axis] + 1, sizes[axis]) for axis in sizes}
    down = {axis: lax.rem(place[axis] + sizes[axis] - 1, sizes[axis]) for axis in sizes}

    def pair(axis, first, last, low, high, slot):
        return [
            pltpu.make_async_remote_copy(
                src_ref=source,
                dst_ref=landing,
                send_sem=edge_sem.at[slot + i],
                recv_sem=edge_recv.at[slot + i],
                device_id=device(axis, target[axis]),
                device_id_type=pl.DeviceIdType.MESH,
            )
            for i, (source, landing, target) in enumerate(((last, low, up), (first, high, down)))
        ]

    stress_rows = []
    for k, c in enumerate(sources[0]):
        stress_rows += pair(
            "bx",
            stress_ref.at[c, :, pl.ds(0, 8), :],
            stress_ref.at[c, :, pl.ds(cells - 8, 8), :],
            row_in.at[0, k],
            row_in.at[1, k],
            2 * k,
        )
    stress_cols = pair("by", col_out.at[0], col_out.at[1], col_in.at[0], col_in.at[1], 6)
    deep = pl.ds(1, layers - 1)
    deep_rows, top_rows = [
        pair(
            "bx",
            v_held.at[:, z, pl.ds(0, 8), :],
            v_held.at[:, z, pl.ds(cells - 8, 8), :],
            row_ref.at[0, :, z],
            row_ref.at[1, :, z],
            slot,
        )
        for z, slot in ((deep, 8), (0, 12))
    ]
    top_cols = pair("by", top_out.at[0], top_out.at[1], top_in.at[0], top_in.at[1], 14)
    new_cols = pair("by", col_new.at[0], col_new.at[1], col_ref.at[0], col_ref.at[1], 10)
    sides = (pl.ds(0, block), pl.ds(width - block, block))
    edge_loads = [
        pltpu.make_async_copy(
            stress_ref.at[c, :, :, side], edge_held.at[i, k], slab_sem.at[3 * i + k]
        )
        for i, side in enumerate(sides)
        for k, c in enumerate(sources[1])
    ]
    velocity_load = pltpu.make_async_copy(velocity_ref, v_held, slab_sem.at[6])
    deep_store = pltpu.make_async_copy(v_held.at[:, deep], v_ref.at[:, deep], slab_sem.at[7])
    top_store = pltpu.make_async_copy(v_held.at[:, 0], v_ref.at[:, 0], slab_sem.at[8])

    def tile_loads(t):
        slot = lax.rem(t, 2)
        row = pl.multiple_of(t * size, 8)
        before = pl.multiple_of(jnp.maximum(row - 8, 0), 8)
        after = pl.multiple_of(jnp.minimum(row + size, cells - 8), 8)
        loads = [
            pltpu.make_async_copy(
                stress_ref.at[:, :, pl.ds(row, size), :],
                stress_held.at[slot, :, :, pl.ds(8, size), :],
                tile_sem.at[slot, 0],
            )
        ]
        for k, c in enumerate(sources[0]):
            for i, (source, landing) in enumerate(((before, 0), (after, size + 8))):
                loads.append(
                    pltpu.make_async_copy(
                        stress_ref.at[c, :, pl.ds(source, 8), :],
                        stress_held.at[slot, c, :, pl.ds(landing, 8), :],
                        tile_sem.at[slot, 1 + 2 * k + i],
                    )
                )
        return loads

    def edges():
        for load in edge_loads:
            load.wait()
        for k in range(3):
            for z in range(layers):
                lane = pl.ds(k * layers + z, 1)
                col_out[0, :, lane] = edge_held[0, k, z, :, 0:1]
                col_out[1, :, lane] = edge_held[1, k, z, :, block - 1 : block]
        for c in stress_cols:
            c.start()

    def slab(t):
        @pl.when(t == 0)
        def _():
            velocity_load.wait()
            for c in stress_rows + stress_cols:
                c.wait_recv()

        @pl.when(t + 1 < tiles)
        def _():
            for load in tile_loads(t + 1):
                load.start()

        for load in tile_loads(t):
            load.wait()
        slot = lax.rem(t, 2)
        rows = pl.ds(pl.multiple_of(t * size, 8), size)
        for component, (sx, sy, sz) in enumerate(sources):
            for z in range(layers):
                k = component * layers + z
                before = jnp.where(t == 0, row_in[0, component, z, 7:8, :], stress_held[slot, sx, z, 7:8, :])
                after = jnp.where(
                    t == tiles - 1,
                    row_in[1, component, z, 0:1, :],
                    stress_held[slot, sx, z, size + 8 : size + 9, :],
                )
                total = rows_diff(stress_held[slot, sx, z, 8 : size + 8, :], before, after)
                total = total + cols_diff(
                    stress_held[slot, sy, z, 8 : size + 8, :],
                    col_in[0, rows, k : k + 1],
                    col_in[1, rows, k : k + 1],
                )
                if z + 1 < layers:
                    total = total + 0.5 * stress_held[slot, sz, z + 1, 8 : size + 8, :]
                if z > 0:
                    total = total - 0.5 * stress_held[slot, sz, z - 1, 8 : size + 8, :]
                value = v_held[component, z, rows, :] + COURANT * total
                v_held[component, z, rows, :] = value
                if z > 0:
                    col_new[0, rows, k : k + 1] = value[:, 0:1]
                    col_new[1, rows, k : k + 1] = value[:, width - 1 : width]

        @pl.when(t == tiles - 1)
        def _():
            deep_store.start()
            for c in deep_rows + new_cols:
                c.start()

    go(0, 0)
    go(0, 1)
    for load in edge_loads:
        load.start()
    for c in stress_rows:
        c.start()
    velocity_load.start()
    for load in tile_loads(0):
        load.start()
    turns = turns_ref[strike]
    strike_tw_ref[...] = jnp.concatenate([turns, jnp.zeros((block - 8, cells), F32)], axis=0).T
    first_tile = 3
    first_back = count + 1
    gap = first_back + parts

    def turn_of(s):
        last, none = components - 1, components
        whole = lax.rem(s + parts - 1, parts) == 0
        step = lax.div(s - 1, parts)
        now = jnp.where(jnp.logical_and(whole, step >= 2), step - 2, none)
        now = jnp.where(now >= last, none, now)
        now = jnp.where(s == gap, last, now)
        early = jnp.where(s == 0, 0, none)
        early = jnp.where(s == first_back + 1, 1, early)
        early = jnp.where(s == gap + 1, 2, early)
        return jnp.where(forward, now, early)

    @pl.loop(0, first_back + count + 2)
    def _(s):
        @pl.when(s < count)
        def _():
            enter(s)

        @pl.when(s + 2 < count)
        def _():
            go(0, s + 2)

        @pl.when(jnp.logical_and(forward, s == 2 * parts + 1))
        def _():
            weigh()

        @pl.when(s == 0)
        def _():
            edges()

        @pl.when(s == 0)
        def _():
            for load in lag_loads:
                load.wait()

        @pl.when(jnp.logical_and(s == 0, jnp.logical_not(full)))
        def _():
            mirrored()
            swap.start()

        @pl.when(s < components)
        def _():
            remember(2 * s)
            remember(2 * s + 1)

        turn = turn_of(s)

        @pl.when(turn < components)
        def _():
            respond(turn)

        @pl.when(jnp.logical_and(s > 0, s <= count))
        def _():
            across(s - 1)

        turned = s - first_back - (s > gap).astype(jnp.int32)

        @pl.when(jnp.logical_and(jnp.logical_and(turned >= 0, turned < count), s != gap))
        def _():
            back(turned)

        done = s - first_back - 1 - (s > gap + 1).astype(jnp.int32)

        @pl.when(jnp.logical_and(jnp.logical_and(done >= 0, done < count), s != gap + 1))
        def _():
            leave(done)

        @pl.when(jnp.logical_and(s >= first_tile, s < tiles + first_tile))
        def _():
            slab(s - first_tile)

    @pl.when(jnp.logical_not(forward))
    def _():
        swap.wait_send()

    @pl.loop(0, count)
    def _(g):
        take(5, g)
        spread_end(g)
        c = lax.div(g, parts)
        lanes = pl.ds(pl.multiple_of(lax.rem(g, parts) * narrow, narrow), narrow)
        high = cells // sizes["bx"]
        for b in range(sizes["bx"]):
            rows = pl.ds(b * high, high)
            v_held[c, 0, rows, lanes] = v_held[c, 0, rows, lanes] - (0.5 * COURANT) * o_ref[c, b, :, lanes]

    for c in top_rows:
        c.start()
    top_store.start()
    lane = lax.broadcasted_iota(jnp.int32, (cells, block), 1)
    for i, side in enumerate((0, width - block)):
        at = block - 1 if i else 0
        total = jnp.zeros((cells, block), F32)
        for c in range(components):
            value = v_held[c, 0, :, side : side + block][:, at : at + 1]
            total = jnp.where(lane == c, value, total)
        top_out[i] = total.T[:8]
    for c in top_cols:
        c.start()
    for c in new_cols + deep_rows + top_cols:
        c.wait_recv()
    for i in range(2):
        filled = jnp.concatenate([top_in[i], jnp.zeros((block - 8, cells), F32)], axis=0).T
        for c in range(components):
            col_ref[i, :, c * layers : c * layers + 1] = filled[:, c : c + 1]
    deep_store.wait()
    top_store.wait()
    for c in stress_rows + stress_cols + new_cols + deep_rows + top_cols:
        c.wait_send()
    for c in top_rows:
        c.wait()


def fault_velocity(interface, kernel, history, tables, velocity, stress, scale):
    strike_count, dip_count = lax.axis_size("bx"), lax.axis_size("by")
    count, cells, width = interface.shape
    rows, modes = cells // strike_count, cells // dip_count
    parts = 2 if width % 256 == 0 else 1
    narrow = width // parts
    face = interface.reshape(count, strike_count, rows, width)
    chunks = count * parts
    flat = (chunks, strike_count, rows, narrow)
    wide = (chunks, strike_count, 2, rows, narrow)
    tall = (chunks, dip_count, 2, modes, narrow)
    layers = velocity.shape[1]
    tile, block = min(32, cells), min(128, width)
    operands = (face, *tables, kernel, history, velocity, stress)
    vmem, anywhere = pl.BlockSpec(memory_space=pltpu.VMEM), pl.BlockSpec(memory_space=pl.ANY)
    return pl.pallas_call(
        partial(fault_kernel, scale),
        out_shape=[
            struct(velocity.shape),
            struct((2, count, layers, 8, width)),
            struct((2, cells, block)),
        ],
        in_specs=[anywhere] + [vmem] * len(tables) + [anywhere] * 4,
        out_specs=[anywhere, vmem, vmem],
        scratch_shapes=[
            *[pltpu.VMEM(s, F32) for s in (flat, wide, wide, tall, tall, tall, tall, wide)],
            pltpu.VMEM((2, cells, width), F32),
            pltpu.VMEM((2, cells, narrow), F32),
            pltpu.VMEM((cells, width), F32),
            pltpu.VMEM((cells, block), F32),
            pltpu.VMEM((kernel.shape[0], cells, width), F32),
            pltpu.VMEM((2, history.shape[0], cells, width), F32),
            pltpu.VMEM((count, 2, cells, width), F32),
            pltpu.SemaphoreType.DMA((dip_count,)),
            pltpu.SemaphoreType.DMA((2, dip_count)),
            pltpu.SemaphoreType.DMA((7, chunks)),
            pltpu.SemaphoreType.DMA((6, chunks)),
            pltpu.SemaphoreType.DMA((2,)),
            pltpu.VMEM(face.shape, F32),
            pltpu.VMEM(velocity.shape, F32),
            pltpu.VMEM((2, 6, layers, tile + 16, width), F32),
            pltpu.VMEM((2, 3, layers, cells, block), F32),
            pltpu.VMEM((2, 3, layers, 8, width), F32),
            pltpu.VMEM((2, cells, block), F32),
            pltpu.VMEM((2, cells, block), F32),
            pltpu.VMEM((2, cells, block), F32),
            pltpu.VMEM((2, 8, cells), F32),
            pltpu.VMEM((2, 8, cells), F32),
            pltpu.SemaphoreType.DMA((9,)),
            pltpu.SemaphoreType.DMA((2, 7)),
            pltpu.SemaphoreType.DMA((16,)),
            pltpu.SemaphoreType.DMA((16,)),
        ],
        compiler_params=pltpu.CompilerParams(
            collective_id=0, has_side_effects=True, vmem_limit_bytes=63 * 1024 * 1024
        ),
        name="fault_velocity",
    )(*operands)


def tile_spec(shape, tile):
    block = shape[:-2] + (tile, shape[-1])
    lead = (0,) * (len(shape) - 2)
    return pl.BlockSpec(block, lambda i: lead + (i, 0))


def halo_specs(shape, tile):
    block = shape[:-2] + (8, shape[-1])
    lead = (0,) * (len(shape) - 2)
    step, last = tile // 8, shape[-2] // 8 - 1
    return [
        pl.BlockSpec(block, lambda i: lead + (jnp.maximum(i * step - 1, 0), 0)),
        pl.BlockSpec(block, lambda i: lead + (jnp.minimum((i + 1) * step, last), 0)),
    ]


def local(interface_velocity, history, kernel, velocity, stress, cohesion):
    strike_count, dip_count = lax.axis_size("bx"), lax.axis_size("by")
    _, layers, cells, width = velocity.shape
    strike_length, dip_length = cells * strike_count, width * dip_count
    scale = 1.0 / math.sqrt(strike_length * dip_length)
    turn = np.outer(np.arange(strike_count), np.arange(cells)) * (2.0 * math.pi / strike_length)
    turns = np.zeros((strike_count, 8, cells), np.float32)
    turns[:, 0], turns[:, 1] = np.cos(turn), np.sin(turn)
    lane = np.outer(np.arange(dip_count), np.arange(width)) * (2.0 * math.pi / dip_length)
    dip_tw = jnp.asarray(np.stack([np.cos(lane), np.sin(lane)]).astype(np.float32))
    dip_table = square_table(width)
    strike_table = square_table(cells)
    tables = (jnp.asarray(turns), strike_table, dip_tw, dip_table)

    velocity_part, rows, cols = fault_velocity(
        interface_velocity, kernel, history, tables, velocity, stress, scale
    )
    tile = min(64, cells)
    return pl.pallas_call(
        stress_step,
        grid=(cells // tile,),
        in_specs=[
            tile_spec(velocity.shape, tile),
            *halo_specs(velocity.shape, tile),
            whole_block(rows.shape),
            tile_spec(cols.shape, tile),
            tile_spec(interface_velocity.shape, tile),
            tile_spec(stress.shape, tile),
            tile_spec(cohesion.shape, tile),
        ],
        out_specs=[tile_spec(velocity.shape, tile), tile_spec(stress.shape, tile)],
        out_shape=[struct(velocity.shape), struct(stress.shape)],
        cost_estimate=cost(2e7, stress, stress, velocity),
        name="stress_step",
    )(velocity_part, velocity_part, velocity_part, rows, cols, interface_velocity, stress, cohesion)


def solution(mesh):
    return jax.shard_map(
        local,
        mesh=mesh,
        in_specs=(
            P(None, "bx", "by"),
            P(None, None, None, "by", "bx", None, None),
            P(None, "by", "bx", None, None),
            P(None, None, "bx", "by"),
            P(None, None, "bx", "by"),
            P(None, "bx", "by"),
        ),
        out_specs=(P(None, None, "bx", "by"), P(None, None, "bx", "by")),
        check_vma=False,
    )
```

```python
from functools import partial
import math

import jax
import jax.numpy as jnp
import numpy as np
from jax import lax
from jax.experimental import pallas as pl
from jax.experimental.pallas import tpu as pltpu
from jax.sharding import PartitionSpec as P

COURANT = 0.3
FRICTION = 0.6
F32 = jnp.float32
BF16 = jnp.bfloat16


def halves(table):
    high = np.asarray(table, np.float32).astype(BF16)
    low = (np.asarray(table, np.float64) - high.astype(np.float64)).astype(BF16)
    return np.stack([high, low])


def square_table(length):
    index = np.arange(length)
    angle = 2.0 * math.pi / length * (index[:, None] * index[None, :] % length)
    return jnp.asarray(np.stack([halves(np.cos(angle)), halves(np.sin(angle))]))


def split(value):
    high = value.astype(BF16)
    return high, (value - high.astype(F32)).astype(BF16)


def product(value, table, left):
    def dot(a, b):
        if left:
            a, b = b, a
        return lax.dot_general(a, b, (((1,), (0,)), ((), ())), preferred_element_type=F32)

    return dot(value[0], table[0]) + (dot(value[0], table[1]) + dot(value[1], table[0]))


def complex_product(real_part, imag_part, table_ref, sign, left):
    cos = (table_ref[0, 0], table_ref[0, 1])
    sin = (table_ref[1, 0], table_ref[1, 1])
    real_part, imag_part = split(real_part), split(imag_part)
    return (
        product(real_part, cos, left) - sign * product(imag_part, sin, left),
        product(imag_part, cos, left) + sign * product(real_part, sin, left),
    )


def root(index, count):
    angle = 2.0 * math.pi * (index % count) / count
    cos, sin = math.cos(angle), math.sin(angle)
    return [float(round(v)) if abs(v - round(v)) < 1e-12 else v for v in (cos, sin)]


def add_term(total, factor, value):
    if factor == 0.0:
        return total
    term = value if factor == 1.0 else (-value if factor == -1.0 else factor * value)
    return term if total is None else total + term


def strike_forward(count, x_ref, o_ref):
    for r in range(count):
        real_part = imag_part = None
        for b in range(count):
            cos, sin = root(r * b, count)
            real_part = add_term(real_part, cos, x_ref[b])
            imag_part = add_term(imag_part, -sin, x_ref[b])
        o_ref[r, 0] = real_part
        o_ref[r, 1] = jnp.zeros_like(real_part) if imag_part is None else imag_part


def strike_inverse(count, scale, x_ref, o_ref):
    for b in range(count):
        total = None
        for r in range(count):
            cos, sin = root(r * b, count)
            total = add_term(total, cos, x_ref[r, 0])
            total = add_term(total, -sin, x_ref[r, 1])
        o_ref[b] = scale * total


def strike_cells_dft(sign, x_ref, tw_ref, table_ref, o_ref, held):
    blocks, _, rows, _ = x_ref.shape
    for s in range(blocks):
        for z in range(2):
            held[z, pl.ds(s * rows, rows), :] = x_ref[s, z]
    cos, sin = tw_ref[:, 0:1], sign * tw_ref[:, 1:2]
    real_part, imag_part = held[0], held[1]
    if sign < 0:
        real_part, imag_part = (
            real_part * cos - imag_part * sin,
            real_part * sin + imag_part * cos,
        )
    real_part, imag_part = complex_product(real_part, imag_part, table_ref, sign, True)
    if sign > 0:
        real_part, imag_part = (
            real_part * cos - imag_part * sin,
            real_part * sin + imag_part * cos,
        )
    held[0] = real_part
    held[1] = imag_part
    blocks, _, rows, _ = o_ref.shape
    for s in range(blocks):
        for z in range(2):
            o_ref[s, z] = held[z, pl.ds(s * rows, rows), :]


def dip_forward(x_refs, tw_ref, table_ref, weight_ref, past_ref, held):
    count, _, rows, width = x_refs[0].shape
    for h, x_ref in enumerate(x_refs):
        part = slice(h * width, (h + 1) * width)
        for l in range(count):
            real_part = imag_part = None
            for j in range(count):
                cos, sin = root(l * j, count)
                real_part = add_term(real_part, cos, x_ref[j, 0])
                real_part = add_term(real_part, sin, x_ref[j, 1])
                imag_part = add_term(imag_part, cos, x_ref[j, 1])
                imag_part = add_term(imag_part, -sin, x_ref[j, 0])
            cos, sin = tw_ref[0, l : l + 1, part], tw_ref[1, l : l + 1, part]
            held[0, pl.ds(l * rows, rows), part] = real_part * cos + imag_part * sin
            held[1, pl.ds(l * rows, rows), part] = imag_part * cos - real_part * sin
    real_part, imag_part = complex_product(held[0], held[1], table_ref, -1.0, False)
    weight = weight_ref[...]
    held[0] = weight * real_part + past_ref[0]
    held[1] = weight * imag_part + past_ref[1]


def dip_inverse(held, tw_ref, table_ref, o_refs):
    count, _, rows, width = o_refs[0].shape
    real_part, imag_part = complex_product(held[0], held[1], table_ref, 1.0, False)
    held[0] = real_part
    held[1] = imag_part
    for l in range(count):
        cos, sin = tw_ref[0, l : l + 1, :], tw_ref[1, l : l + 1, :]
        real_part = held[0, pl.ds(l * rows, rows), :]
        imag_part = held[1, pl.ds(l * rows, rows), :]
        held[0, pl.ds(l * rows, rows), :] = real_part * cos - imag_part * sin
        held[1, pl.ds(l * rows, rows), :] = imag_part * cos + real_part * sin
    for h, o_ref in enumerate(o_refs):
        part = slice(h * width, (h + 1) * width)
        for j in range(count):
            real_part = imag_part = None
            for l in range(count):
                cos, sin = root(l * j, count)
                lr = held[0, pl.ds(l * rows, rows), part]
                li = held[1, pl.ds(l * rows, rows), part]
                real_part = add_term(real_part, cos, lr)
                real_part = add_term(real_part, -sin, li)
                imag_part = add_term(imag_part, cos, li)
                imag_part = add_term(imag_part, sin, lr)
            o_ref[j, 0] = real_part
            o_ref[j, 1] = imag_part


def rows_diff(value, before, after):
    count = value.shape[0]
    row = lax.broadcasted_iota(jnp.int32, value.shape, 0)
    low = jnp.where(row == 0, before, pltpu.roll(value, 1, 0))
    high = jnp.where(row == count - 1, after, pltpu.roll(value, count - 1, 0))
    return high - low


def cols_diff(value, before, after):
    count = value.shape[1]
    col = lax.broadcasted_iota(jnp.int32, value.shape, 1)
    low = jnp.where(col == 0, before, pltpu.roll(value, 1, 1))
    high = jnp.where(col == count - 1, after, pltpu.roll(value, count - 1, 1))
    return high - low


def stress_step(v_ref, prev_ref, next_ref, row_ref, col_ref, w_ref, s_ref, y_ref, n_ref, o_ref):
    layers = v_ref.shape[1]
    i, last = pl.program_id(0), pl.num_programs(0) - 1
    n_ref[...] = v_ref[...]
    for z in range(layers):
        dx, dy, dz = [], [], []
        for c in range(3):
            before = jnp.where(i == 0, row_ref[0, c, z, 7:8, :], prev_ref[c, z, 7:8, :])
            after = jnp.where(i == last, row_ref[1, c, z, 0:1, :], next_ref[c, z, 0:1, :])
            k = c * layers + z
            dx.append(rows_diff(v_ref[c, z], before, after))
            dy.append(
                cols_diff(v_ref[c, z], col_ref[0, :, k : k + 1], col_ref[1, :, k : k + 1])
            )
            low = w_ref[c] if z == 0 else v_ref[c, z - 1]
            if z + 1 < layers:
                dz.append(v_ref[c, z + 1] - low)
            else:
                dz.append(-low)
        step = 0.5 * COURANT
        dilation = dx[0] + dy[1] + dz[2]
        xx = s_ref[0, z] + step * (dilation + 2.0 * dx[0])
        yy = s_ref[1, z] + step * (dilation + 2.0 * dy[1])
        zz = s_ref[2, z] + step * (dilation + 2.0 * dz[2])
        xy = s_ref[3, z] + step * (dy[0] + dx[1])
        xz = s_ref[4, z] + step * (dz[0] + dx[2])
        yz = s_ref[5, z] + step * (dz[1] + dy[2])
        pressure = (xx + yy + zz) * (1.0 / 3.0)
        xx, yy, zz = xx - pressure, yy - pressure, zz - pressure
        shear = jnp.sqrt(0.5 * (xx * xx + yy * yy + zz * zz) + (xy * xy + xz * xz + yz * yz))
        limit = y_ref[z] + FRICTION * jnp.maximum(-pressure, 0.0)
        factor = limit / jnp.maximum(shear, limit)
        o_ref[0, z] = pressure + factor * xx
        o_ref[1, z] = pressure + factor * yy
        o_ref[2, z] = pressure + factor * zz
        o_ref[3, z] = factor * xy
        o_ref[4, z] = factor * xz
        o_ref[5, z] = factor * yz


def whole_block(shape):
    return pl.BlockSpec(shape, lambda *_: (0,) * len(shape))


def struct(shape):
    return jax.ShapeDtypeStruct(shape, F32)


def cost(flops, *arrays):
    moved = sum(math.prod(a.shape) * a.dtype.itemsize for a in arrays)
    return pl.CostEstimate(flops=int(flops), bytes_accessed=int(moved), transcendentals=0)


def fault_kernel(
    scale,
    face_ref,
    turns_ref,
    strike_table_ref,
    dip_tw_ref,
    dip_table_ref,
    kernel_ref,
    history_ref,
    velocity_ref,
    stress_ref,
    v_ref,
    row_ref,
    col_ref,
    x1,
    b1,
    b2,
    t1,
    t2,
    u1,
    u2,
    w2,
    held,
    held_part,
    weight,
    strike_tw_ref,
    lags,
    lag_held,
    past_ref,
    lag_sem,
    past_sem,
    send_sem,
    recv_sem,
    mirror_sem,
    o_ref,
    v_held,
    stress_held,
    edge_held,
    row_in,
    col_out,
    col_in,
    col_new,
    top_out,
    top_in,
    slab_sem,
    tile_sem,
    edge_sem,
    edge_recv,
):
    count, narrow = x1.shape[0], x1.shape[-1]
    w1, y1, now_ref = b1, x1, lags.at[0]
    parts = count // past_ref.shape[0]
    sizes = {"bx": lax.axis_size("bx"), "by": lax.axis_size("by")}
    place = {"bx": lax.axis_index("bx"), "by": lax.axis_index("by")}

    def device(axis, target):
        if axis == "bx":
            return (target, place["by"])
        return (place["bx"], target)

    strike, dip = place["bx"], place["by"]
    modes, zone = t2.shape[3], min(8, t2.shape[3])

    def active(target):
        return lax.rem(strike + target, 2) == 0

    full = active(dip)
    thin = jnp.logical_and(jnp.logical_not(full), strike == 0)
    forward = jnp.logical_or(full, strike == 0)
    mirror = (lax.rem(sizes["bx"] - strike, sizes["bx"]), sizes["by"] - 1 - dip)

    layers, cells, width = v_held.shape[1:]
    components = past_ref.shape[0]
    lag_loads = [
        pltpu.make_async_copy(
            kernel_ref.at[:, :, 0, l, :], lags.at[:, pl.ds(l * modes, modes), :], lag_sem.at[l]
        )
        for l in range(sizes["by"])
    ]

    def past_loads(i):
        slot = lax.rem(i, 2)
        return [
            pltpu.make_async_copy(
                history_ref.at[:, slot, lax.div(i, 2), :, 0, l, :],
                lag_held.at[slot, :, pl.ds(l * modes, modes), :],
                past_sem.at[slot, l],
            )
            for l in range(sizes["by"])
        ]

    for load in lag_loads:
        load.start()
    barrier = pltpu.get_barrier_semaphore()
    pl.semaphore_signal(barrier, 1, device_id=mirror, device_id_type=pl.DeviceIdType.MESH)
    for axis in ("bx", "by"):

        @pl.loop(1, sizes[axis])
        def _(k):
            target = lax.rem(place[axis] + k, sizes[axis])
            pl.semaphore_signal(
                barrier, 1, device_id=device(axis, target), device_id_type=pl.DeviceIdType.MESH
            )

    pl.semaphore_wait(barrier, sizes["bx"] + sizes["by"] - 1)

    swap = pltpu.make_async_remote_copy(
        src_ref=weight,
        dst_ref=weight,
        send_sem=mirror_sem.at[0],
        recv_sem=mirror_sem.at[1],
        device_id=mirror,
        device_id_type=pl.DeviceIdType.MESH,
    )


    def piece(ref, g, slot):
        if len(ref.shape) == 4 and ref.shape[0] != count:
            return ref.at[g // parts, slot, :, pl.ds(pl.multiple_of(g % parts * narrow, narrow), narrow)]
        if ref is face_ref or ref is o_ref:
            return ref.at[g, slot, :, pl.ds(0, narrow)]
        return ref.at[g, slot]

    def several(ref, g, number):
        if len(ref.shape) == 4 and ref.shape[0] != count:
            lanes = pl.ds(pl.multiple_of(g % parts * narrow, narrow), narrow)
            return ref.at[g // parts, pl.ds(0, number), :, lanes]
        return ref.at[g, pl.ds(0, number)]

    def settle(ref, sem):
        pltpu.make_async_copy(ref, ref, sem).wait()

    def copy(stage, axis, c, k, source, landing):
        me = place[axis]
        target = lax.rem(me + k, sizes[axis])
        return pltpu.make_async_remote_copy(
            src_ref=piece(source, c, target),
            dst_ref=piece(landing, c, me),
            send_sem=send_sem.at[stage, c],
            recv_sem=recv_sem.at[stage, c],
            device_id=device(axis, target),
            device_id_type=pl.DeviceIdType.MESH,
        )

    def own(stage, axis, c, source, landing):
        me = place[axis]
        return pltpu.make_async_copy(
            piece(source, c, me), piece(landing, c, me), recv_sem.at[stage, c]
        )

    def send(stage, axis, c, source, landing):
        @pl.loop(1, sizes[axis])
        def _(k):
            copy(stage, axis, c, k, source, landing).start()

        own(stage, axis, c, source, landing).start()

    def receive(stage, axis, c, source, landing):
        settle(several(landing, c, sizes[axis]), recv_sem.at[stage, c])

    def tile(ref, g, slot):
        return ref.at[g, slot, :, pl.ds(0, zone), :]

    def lean(g, k):
        target = lax.rem(dip + k, sizes["by"])
        return pltpu.make_async_remote_copy(
            src_ref=tile(t1, g, target),
            dst_ref=tile(t2, g, dip),
            send_sem=send_sem.at[6, g],
            recv_sem=recv_sem.at[2, g],
            device_id=device("by", target),
            device_id_type=pl.DeviceIdType.MESH,
        )

    def lean_own(g):
        return pltpu.make_async_copy(tile(t1, g, dip), tile(t2, g, dip), recv_sem.at[2, g])

    def spread(g):
        @pl.loop(1, sizes["by"])
        def _(k):
            wanted = active(lax.rem(dip + k, sizes["by"]))

            @pl.when(wanted)
            def _():
                copy(2, "by", g, k, t1, t2).start()

            @pl.when(jnp.logical_and(jnp.logical_not(wanted), strike == 0))
            def _():
                lean(g, k).start()

        @pl.when(full)
        def _():
            own(2, "by", g, t1, t2).start()

        @pl.when(thin)
        def _():
            lean_own(g).start()

    half = sizes["by"] // 2

    def spread_end(g):
        def wait(condition, number, zoned):
            @pl.when(condition)
            def _():
                if zoned:
                    settle(t1.at[g, pl.ds(0, number), :, pl.ds(0, zone), :], send_sem.at[6, g])
                else:
                    settle(t1.at[g, pl.ds(0, number)], send_sem.at[2, g])

        wait(full, half - 1, False)
        wait(jnp.logical_not(full), half, False)
        wait(jnp.logical_and(full, strike == 0), half, True)
        wait(thin, half - 1, True)

    def gather(g):
        @pl.when(full)
        def _():
            settle(t2.at[g], recv_sem.at[2, g])

        @pl.when(thin)
        def _():
            settle(t2.at[g, :, :, pl.ds(0, zone), :], recv_sem.at[2, g])

    stages = (
        ("bx", face_ref, x1),
        ("bx", b1, b2),
        ("by", t1, t2),
        ("by", u1, u2),
        ("bx", w1, w2),
        ("bx", y1, o_ref),
    )

    def go(stage, g):
        axis, source, landing = stages[stage]
        send(stage, axis, g, source, landing)

    def take(stage, g):
        axis, source, landing = stages[stage]
        receive(stage, axis, g, source, landing)

    def sent(stage, g):
        axis, source, landing = stages[stage]
        settle(several(landing, g, sizes[axis] - 1), send_sem.at[stage, g])

    def enter(g):
        take(0, g)
        strike_forward(sizes["bx"], x1.at[g], b1.at[g])
        go(1, g)

    def across(g):
        take(1, g)
        strike_cells_dft(-1.0, b2.at[g], strike_tw_ref, strike_table_ref, t1.at[g], held_part)
        spread(g)

    def back(g):
        take(3, g)
        sent(1, g)
        strike_cells_dft(1.0, u2.at[g], strike_tw_ref, strike_table_ref, w1.at[g], held_part)
        go(4, g)

    def leave(g):
        take(4, g)
        strike_inverse(sizes["bx"], scale, w2.at[g], y1.at[g])
        go(5, g)

    def remember(i):
        for load in past_loads(i):
            load.wait()
        slot = lax.rem(i, 2)

        @pl.loop(0, cells // 8)
        def _(k):
            rows = pl.ds(pl.multiple_of(k * 8, 8), 8)
            total = lags[1, rows, :] * lag_held[slot, 0, rows, :]
            for h in range(1, lag_held.shape[1]):
                total = total + lags[h + 1, rows, :] * lag_held[slot, h, rows, :]
            past_ref[lax.div(i, 2), slot, rows, :] = total

        @pl.when(i + 2 < 2 * components)
        def _():
            for load in past_loads(i + 2):
                load.start()

    def pick(rows, columns, total, wrap):
        at = lax.broadcasted_iota(jnp.int32, (rows, columns), 0)
        at = at + lax.broadcasted_iota(jnp.int32, (rows, columns), 1)
        at = jnp.where(at == total, 1.0, jnp.where(at == wrap, 1.0, 0.0))
        return at.astype(BF16)

    def place_all(value, table, left):
        total = None
        for _ in range(3):
            piece = value.astype(BF16)
            value = value - piece.astype(F32)
            a, b = (table, piece) if left else (piece, table)
            term = lax.dot_general(a, b, (((1,), (0,)), ((), ())), preferred_element_type=F32)
            total = term if total is None else total + term
        return total

    def mirrored():
        flip = pick(modes, modes, jnp.where(strike == 0, modes, modes - 1), -1)
        for l in range(sizes["by"]):
            other = (sizes["by"] - l) % sizes["by"]
            table = pick(width, width, width if l == 0 else width - 1, 0 if l == 0 else -1)
            value = place_all(now_ref[pl.ds(l * modes, modes), :], table, False)
            weight[pl.ds(other * modes, modes), :] = place_all(value, flip, True)

    def weigh():
        @pl.when(full)
        def _():
            swap.wait_recv()
            weight[...] = scale * (now_ref[...] + weight[...])

        @pl.when(thin)
        def _():
            swap.wait_send()
            if zone < modes:

                @pl.loop(0, count)
                def _(g):
                    t2[g, :, :, pl.ds(zone, modes - zone), :] = jnp.zeros(
                        (*t2.shape[1:3], modes - zone, narrow), F32
                    )

            row = lax.broadcasted_iota(jnp.int32, now_ref.shape, 0)
            weight[...] = jnp.where(lax.rem(row, modes) == 0, scale * now_ref[...], 0.0)

    def respond(c):
        @pl.when(forward)
        def _():
            for h in range(parts):
                gather(c * parts + h)
            dip_forward(
                [t2.at[c * parts + h] for h in range(parts)],
                dip_tw_ref,
                dip_table_ref,
                weight,
                past_ref.at[c],
                held,
            )

        @pl.when(jnp.logical_not(forward))
        def _():
            held[...] = past_ref[c]

        dip_inverse(
            held,
            dip_tw_ref,
            dip_table_ref,
            [u1.at[c * parts + h] for h in range(parts)],
        )
        for h in range(parts):
            go(3, c * parts + h)

    for load in past_loads(0) + past_loads(1):
        load.start()
    size = stress_held.shape[3] - 16
    tiles = cells // size
    block = col_out.shape[2]
    sources = ((0, 3, 4), (3, 1, 5), (4, 5, 2))
    up = {axis: lax.rem(place[axis] + 1, sizes[axis]) for axis in sizes}
    down = {axis: lax.rem(place[axis] + sizes[axis] - 1, sizes[axis]) for axis in sizes}

    def pair(axis, first, last, low, high, slot):
        return [
            pltpu.make_async_remote_copy(
                src_ref=source,
                dst_ref=landing,
                send_sem=edge_sem.at[slot + i],
                recv_sem=edge_recv.at[slot + i],
                device_id=device(axis, target[axis]),
                device_id_type=pl.DeviceIdType.MESH,
            )
            for i, (source, landing, target) in enumerate(((last, low, up), (first, high, down)))
        ]

    stress_rows = []
    for k, c in enumerate(sources[0]):
        stress_rows += pair(
            "bx",
            stress_ref.at[c, :, pl.ds(0, 8), :],
            stress_ref.at[c, :, pl.ds(cells - 8, 8), :],
            row_in.at[0, k],
            row_in.at[1, k],
            2 * k,
        )
    stress_cols = pair("by", col_out.at[0], col_out.at[1], col_in.at[0], col_in.at[1], 6)
    deep = pl.ds(1, layers - 1)
    deep_rows, top_rows = [
        pair(
            "bx",
            v_held.at[:, z, pl.ds(0, 8), :],
            v_held.at[:, z, pl.ds(cells - 8, 8), :],
            row_ref.at[0, :, z],
            row_ref.at[1, :, z],
            slot,
        )
        for z, slot in ((deep, 8), (0, 12))
    ]
    top_cols = pair("by", top_out.at[0], top_out.at[1], top_in.at[0], top_in.at[1], 14)
    new_cols = pair("by", col_new.at[0], col_new.at[1], col_ref.at[0], col_ref.at[1], 10)
    sides = (pl.ds(0, block), pl.ds(width - block, block))
    edge_loads = [
        pltpu.make_async_copy(
            stress_ref.at[c, :, :, side], edge_held.at[i, k], slab_sem.at[3 * i + k]
        )
        for i, side in enumerate(sides)
        for k, c in enumerate(sources[1])
    ]
    velocity_load = pltpu.make_async_copy(velocity_ref, v_held, slab_sem.at[6])
    deep_store = pltpu.make_async_copy(v_held.at[:, deep], v_ref.at[:, deep], slab_sem.at[7])
    top_store = pltpu.make_async_copy(v_held.at[:, 0], v_ref.at[:, 0], slab_sem.at[8])

    def tile_loads(t):
        slot = lax.rem(t, 2)
        row = pl.multiple_of(t * size, 8)
        before = pl.multiple_of(jnp.maximum(row - 8, 0), 8)
        after = pl.multiple_of(jnp.minimum(row + size, cells - 8), 8)
        loads = [
            pltpu.make_async_copy(
                stress_ref.at[:, :, pl.ds(row, size), :],
                stress_held.at[slot, :, :, pl.ds(8, size), :],
                tile_sem.at[slot, 0],
            )
        ]
        for k, c in enumerate(sources[0]):
            for i, (source, landing) in enumerate(((before, 0), (after, size + 8))):
                loads.append(
                    pltpu.make_async_copy(
                        stress_ref.at[c, :, pl.ds(source, 8), :],
                        stress_held.at[slot, c, :, pl.ds(landing, 8), :],
                        tile_sem.at[slot, 1 + 2 * k + i],
                    )
                )
        return loads

    def edges():
        for load in edge_loads:
            load.wait()
        for k in range(3):
            for z in range(layers):
                lane = pl.ds(k * layers + z, 1)
                col_out[0, :, lane] = edge_held[0, k, z, :, 0:1]
                col_out[1, :, lane] = edge_held[1, k, z, :, block - 1 : block]
        for c in stress_cols:
            c.start()

    def slab(t):
        @pl.when(t == 0)
        def _():
            velocity_load.wait()
            for c in stress_rows + stress_cols:
                c.wait_recv()

        @pl.when(t + 1 < tiles)
        def _():
            for load in tile_loads(t + 1):
                load.start()

        for load in tile_loads(t):
            load.wait()
        slot = lax.rem(t, 2)
        rows = pl.ds(pl.multiple_of(t * size, 8), size)
        for component, (sx, sy, sz) in enumerate(sources):
            for z in range(layers):
                k = component * layers + z
                before = jnp.where(t == 0, row_in[0, component, z, 7:8, :], stress_held[slot, sx, z, 7:8, :])
                after = jnp.where(
                    t == tiles - 1,
                    row_in[1, component, z, 0:1, :],
                    stress_held[slot, sx, z, size + 8 : size + 9, :],
                )
                total = rows_diff(stress_held[slot, sx, z, 8 : size + 8, :], before, after)
                total = total + cols_diff(
                    stress_held[slot, sy, z, 8 : size + 8, :],
                    col_in[0, rows, k : k + 1],
                    col_in[1, rows, k : k + 1],
                )
                if z + 1 < layers:
                    total = total + stress_held[slot, sz, z + 1, 8 : size + 8, :]
                if z > 0:
                    total = total - stress_held[slot, sz, z - 1, 8 : size + 8, :]
                value = v_held[component, z, rows, :] + (0.5 * COURANT) * total
                v_held[component, z, rows, :] = value
                if z > 0:
                    col_new[0, rows, k : k + 1] = value[:, 0:1]
                    col_new[1, rows, k : k + 1] = value[:, width - 1 : width]

        @pl.when(t == tiles - 1)
        def _():
            deep_store.start()
            for c in deep_rows + new_cols:
                c.start()

    go(0, 0)
    go(0, 1)
    for load in edge_loads:
        load.start()
    velocity_load.start()
    for load in tile_loads(0):
        load.start()
    turns = turns_ref[strike]
    strike_tw_ref[...] = jnp.concatenate([turns, jnp.zeros((block - 8, cells), F32)], axis=0).T
    first_tile = 3
    first_back = count + 1
    gap = first_back + parts

    def turn_of(s):
        last, none = components - 1, components
        whole = lax.rem(s + parts - 1, parts) == 0
        step = lax.div(s - 1, parts)
        now = jnp.where(jnp.logical_and(whole, step >= 2), step - 2, none)
        now = jnp.where(now >= last, none, now)
        now = jnp.where(s == gap, last, now)
        early = jnp.where(s == 0, 0, none)
        early = jnp.where(s == first_back + 1, 1, early)
        early = jnp.where(s == gap + 1, 2, early)
        return jnp.where(forward, now, early)

    @pl.loop(0, first_back + count + 2)
    def _(s):
        @pl.when(s < count)
        def _():
            enter(s)

        @pl.when(s + 2 < count)
        def _():
            go(0, s + 2)

        @pl.when(jnp.logical_and(forward, s == 2 * parts + 1))
        def _():
            weigh()

        @pl.when(s == 0)
        def _():
            edges()

        @pl.when(s == 0)
        def _():
            for load in lag_loads:
                load.wait()

        @pl.when(jnp.logical_and(s == 0, jnp.logical_not(full)))
        def _():
            mirrored()
            swap.start()

        @pl.when(s < components)
        def _():
            remember(2 * s)
            remember(2 * s + 1)

        turn = turn_of(s)

        @pl.when(turn < components)
        def _():
            respond(turn)

        @pl.when(jnp.logical_and(s > 0, s <= count))
        def _():
            across(s - 1)

        @pl.when(s == 1)
        def _():
            for c in stress_rows:
                c.start()

        turned = s - first_back - (s > gap).astype(jnp.int32)

        @pl.when(jnp.logical_and(jnp.logical_and(turned >= 0, turned < count), s != gap))
        def _():
            back(turned)

        done = s - first_back - 1 - (s > gap + 1).astype(jnp.int32)

        @pl.when(jnp.logical_and(jnp.logical_and(done >= 0, done < count), s != gap + 1))
        def _():
            leave(done)

        @pl.when(jnp.logical_and(s >= first_tile, s < tiles + first_tile))
        def _():
            slab(s - first_tile)

    @pl.when(jnp.logical_not(forward))
    def _():
        swap.wait_send()

    @pl.loop(0, count)
    def _(g):
        take(5, g)
        c = lax.div(g, parts)
        lanes = pl.ds(pl.multiple_of(lax.rem(g, parts) * narrow, narrow), narrow)
        high = cells // sizes["bx"]
        for b in range(sizes["bx"]):
            rows = pl.ds(b * high, high)
            v_held[c, 0, rows, lanes] = v_held[c, 0, rows, lanes] - (0.5 * COURANT) * o_ref[c, b, :, lanes]

    for c in top_rows:
        c.start()
    top_store.start()
    lane = lax.broadcasted_iota(jnp.int32, (cells, block), 1)
    for i, side in enumerate((0, width - block)):
        at = block - 1 if i else 0
        total = jnp.zeros((cells, block), F32)
        for c in range(components):
            value = v_held[c, 0, :, side : side + block][:, at : at + 1]
            total = jnp.where(lane == c, value, total)
        top_out[i] = total.T[:8]
    for c in top_cols:
        c.start()
    for c in new_cols + deep_rows + top_cols:
        c.wait_recv()
    for i in range(2):
        filled = jnp.concatenate([top_in[i], jnp.zeros((block - 8, cells), F32)], axis=0).T
        for c in range(components):
            col_ref[i, :, c * layers : c * layers + 1] = filled[:, c : c + 1]
    deep_store.wait()
    top_store.wait()
    for c in stress_rows + stress_cols + new_cols + deep_rows + top_cols:
        c.wait_send()

    @pl.loop(0, count)
    def _(g):
        spread_end(g)
        for stage in (0, 3, 4, 5):
            sent(stage, g)

    for c in top_rows:
        c.wait()


def fault_velocity(interface, kernel, history, tables, velocity, stress, scale):
    strike_count, dip_count = lax.axis_size("bx"), lax.axis_size("by")
    count, cells, width = interface.shape
    rows, modes = cells // strike_count, cells // dip_count
    parts = 2 if width % 256 == 0 else 1
    narrow = width // parts
    face = interface.reshape(count, strike_count, rows, width)
    chunks = count * parts
    flat = (chunks, strike_count, rows, narrow)
    wide = (chunks, strike_count, 2, rows, narrow)
    tall = (chunks, dip_count, 2, modes, narrow)
    layers = velocity.shape[1]
    tile, block = min(32, cells), min(128, width)
    operands = (face, *tables, kernel, history, velocity, stress)
    vmem, anywhere = pl.BlockSpec(memory_space=pltpu.VMEM), pl.BlockSpec(memory_space=pl.ANY)
    return pl.pallas_call(
        partial(fault_kernel, scale),
        out_shape=[
            struct(velocity.shape),
            struct((2, count, layers, 8, width)),
            struct((2, cells, block)),
        ],
        in_specs=[anywhere] + [vmem] * len(tables) + [anywhere] * 4,
        out_specs=[anywhere, vmem, vmem],
        scratch_shapes=[
            *[pltpu.VMEM(s, F32) for s in (flat, wide, wide, tall, tall, tall, tall, wide)],
            pltpu.VMEM((2, cells, width), F32),
            pltpu.VMEM((2, cells, narrow), F32),
            pltpu.VMEM((cells, width), F32),
            pltpu.VMEM((cells, block), F32),
            pltpu.VMEM((kernel.shape[0], cells, width), F32),
            pltpu.VMEM((2, history.shape[0], cells, width), F32),
            pltpu.VMEM((count, 2, cells, width), F32),
            pltpu.SemaphoreType.DMA((dip_count,)),
            pltpu.SemaphoreType.DMA((2, dip_count)),
            pltpu.SemaphoreType.DMA((7, chunks)),
            pltpu.SemaphoreType.DMA((6, chunks)),
            pltpu.SemaphoreType.DMA((2,)),
            pltpu.VMEM(face.shape, F32),
            pltpu.VMEM(velocity.shape, F32),
            pltpu.VMEM((2, 6, layers, tile + 16, width), F32),
            pltpu.VMEM((2, 3, layers, cells, block), F32),
            pltpu.VMEM((2, 3, layers, 8, width), F32),
            pltpu.VMEM((2, cells, block), F32),
            pltpu.VMEM((2, cells, block), F32),
            pltpu.VMEM((2, cells, block), F32),
            pltpu.VMEM((2, 8, cells), F32),
            pltpu.VMEM((2, 8, cells), F32),
            pltpu.SemaphoreType.DMA((9,)),
            pltpu.SemaphoreType.DMA((2, 7)),
            pltpu.SemaphoreType.DMA((16,)),
            pltpu.SemaphoreType.DMA((16,)),
        ],
        compiler_params=pltpu.CompilerParams(
            collective_id=0, has_side_effects=True, vmem_limit_bytes=63 * 1024 * 1024
        ),
        name="fault_velocity",
    )(*operands)


def tile_spec(shape, tile):
    block = shape[:-2] + (tile, shape[-1])
    lead = (0,) * (len(shape) - 2)
    return pl.BlockSpec(block, lambda i: lead + (i, 0))


def halo_specs(shape, tile):
    block = shape[:-2] + (8, shape[-1])
    lead = (0,) * (len(shape) - 2)
    step, last = tile // 8, shape[-2] // 8 - 1
    return [
        pl.BlockSpec(block, lambda i: lead + (jnp.maximum(i * step - 1, 0), 0)),
        pl.BlockSpec(block, lambda i: lead + (jnp.minimum((i + 1) * step, last), 0)),
    ]


def local(interface_velocity, history, kernel, velocity, stress, cohesion):
    strike_count, dip_count = lax.axis_size("bx"), lax.axis_size("by")
    _, layers, cells, width = velocity.shape
    strike_length, dip_length = cells * strike_count, width * dip_count
    scale = 1.0 / math.sqrt(strike_length * dip_length)
    turn = np.outer(np.arange(strike_count), np.arange(cells)) * (2.0 * math.pi / strike_length)
    turns = np.zeros((strike_count, 8, cells), np.float32)
    turns[:, 0], turns[:, 1] = np.cos(turn), np.sin(turn)
    lane = np.outer(np.arange(dip_count), np.arange(width)) * (2.0 * math.pi / dip_length)
    dip_tw = jnp.asarray(np.stack([np.cos(lane), np.sin(lane)]).astype(np.float32))
    dip_table = square_table(width)
    strike_table = square_table(cells)
    tables = (jnp.asarray(turns), strike_table, dip_tw, dip_table)

    velocity_part, rows, cols = fault_velocity(
        interface_velocity, kernel, history, tables, velocity, stress, scale
    )
    tile = min(64, cells)
    return pl.pallas_call(
        stress_step,
        grid=(cells // tile,),
        in_specs=[
            tile_spec(velocity.shape, tile),
            *halo_specs(velocity.shape, tile),
            whole_block(rows.shape),
            tile_spec(cols.shape, tile),
            tile_spec(interface_velocity.shape, tile),
            tile_spec(stress.shape, tile),
            tile_spec(cohesion.shape, tile),
        ],
        out_specs=[tile_spec(velocity.shape, tile), tile_spec(stress.shape, tile)],
        out_shape=[struct(velocity.shape), struct(stress.shape)],
        cost_estimate=cost(2e7, stress, stress, velocity),
        name="stress_step",
    )(velocity_part, velocity_part, velocity_part, rows, cols, interface_velocity, stress, cohesion)


def solution(mesh):
    return jax.shard_map(
        local,
        mesh=mesh,
        in_specs=(
            P(None, "bx", "by"),
            P(None, None, None, "by", "bx", None, None),
            P(None, "by", "bx", None, None),
            P(None, None, "bx", "by"),
            P(None, None, "bx", "by"),
            P(None, "bx", "by"),
        ),
        out_specs=(P(None, None, "bx", "by"), P(None, None, "bx", "by")),
        check_vma=False,
    )
```

```python
from functools import partial
import math

import jax
import jax.numpy as jnp
import numpy as np
from jax import lax
from jax.experimental import pallas as pl
from jax.experimental.pallas import tpu as pltpu
from jax.sharding import PartitionSpec as P

COURANT = 0.3
FRICTION = 0.6
F32 = jnp.float32
BF16 = jnp.bfloat16


def halves(table):
    high = np.asarray(table, np.float32).astype(BF16)
    low = (np.asarray(table, np.float64) - high.astype(np.float64)).astype(BF16)
    return np.stack([high, low])


def square_table(length):
    index = np.arange(length)
    angle = 2.0 * math.pi / length * (index[:, None] * index[None, :] % length)
    return jnp.asarray(np.stack([halves(np.cos(angle)), halves(np.sin(angle))]))


def split(value):
    high = value.astype(BF16)
    return high, (value - high.astype(F32)).astype(BF16)


def product(value, table, left):
    def dot(a, b):
        if left:
            a, b = b, a
        return lax.dot_general(a, b, (((1,), (0,)), ((), ())), preferred_element_type=F32)

    return dot(value[0], table[0]) + (dot(value[0], table[1]) + dot(value[1], table[0]))


def complex_product(real_part, imag_part, table_ref, sign, left):
    cos = (table_ref[0, 0], table_ref[0, 1])
    sin = (table_ref[1, 0], table_ref[1, 1])
    real_part, imag_part = split(real_part), split(imag_part)
    return (
        product(real_part, cos, left) - sign * product(imag_part, sin, left),
        product(imag_part, cos, left) + sign * product(real_part, sin, left),
    )


def root(index, count):
    angle = 2.0 * math.pi * (index % count) / count
    cos, sin = math.cos(angle), math.sin(angle)
    return [float(round(v)) if abs(v - round(v)) < 1e-12 else v for v in (cos, sin)]


def add_term(total, factor, value):
    if factor == 0.0:
        return total
    term = value if factor == 1.0 else (-value if factor == -1.0 else factor * value)
    return term if total is None else total + term


def strike_forward(count, x_ref, o_ref):
    for r in range(count):
        real_part = imag_part = None
        for b in range(count):
            cos, sin = root(r * b, count)
            real_part = add_term(real_part, cos, x_ref[b])
            imag_part = add_term(imag_part, -sin, x_ref[b])
        o_ref[r, 0] = real_part
        o_ref[r, 1] = jnp.zeros_like(real_part) if imag_part is None else imag_part


def strike_inverse(count, scale, x_ref, o_ref):
    for b in range(count):
        total = None
        for r in range(count):
            cos, sin = root(r * b, count)
            total = add_term(total, cos, x_ref[r, 0])
            total = add_term(total, -sin, x_ref[r, 1])
        o_ref[b] = scale * total


def strike_cells_dft(sign, x_ref, tw_ref, table_ref, o_ref, held):
    blocks, _, rows, _ = x_ref.shape
    for s in range(blocks):
        for z in range(2):
            held[z, pl.ds(s * rows, rows), :] = x_ref[s, z]
    cos, sin = tw_ref[:, 0:1], sign * tw_ref[:, 1:2]
    real_part, imag_part = held[0], held[1]
    if sign < 0:
        real_part, imag_part = (
            real_part * cos - imag_part * sin,
            real_part * sin + imag_part * cos,
        )
    real_part, imag_part = complex_product(real_part, imag_part, table_ref, sign, True)
    if sign > 0:
        real_part, imag_part = (
            real_part * cos - imag_part * sin,
            real_part * sin + imag_part * cos,
        )
    held[0] = real_part
    held[1] = imag_part
    blocks, _, rows, _ = o_ref.shape
    for s in range(blocks):
        for z in range(2):
            o_ref[s, z] = held[z, pl.ds(s * rows, rows), :]


def dip_forward(x_refs, tw_ref, table_ref, weight_ref, past_ref, held):
    count, _, rows, width = x_refs[0].shape
    for h, x_ref in enumerate(x_refs):
        part = slice(h * width, (h + 1) * width)
        for l in range(count):
            real_part = imag_part = None
            for j in range(count):
                cos, sin = root(l * j, count)
                real_part = add_term(real_part, cos, x_ref[j, 0])
                real_part = add_term(real_part, sin, x_ref[j, 1])
                imag_part = add_term(imag_part, cos, x_ref[j, 1])
                imag_part = add_term(imag_part, -sin, x_ref[j, 0])
            cos, sin = tw_ref[0, l : l + 1, part], tw_ref[1, l : l + 1, part]
            held[0, pl.ds(l * rows, rows), part] = real_part * cos + imag_part * sin
            held[1, pl.ds(l * rows, rows), part] = imag_part * cos - real_part * sin
    real_part, imag_part = complex_product(held[0], held[1], table_ref, -1.0, False)
    weight = weight_ref[...]
    held[0] = weight * real_part + past_ref[0]
    held[1] = weight * imag_part + past_ref[1]


def dip_inverse(held, tw_ref, table_ref, o_refs):
    count, _, rows, width = o_refs[0].shape
    real_part, imag_part = complex_product(held[0], held[1], table_ref, 1.0, False)
    held[0] = real_part
    held[1] = imag_part
    for l in range(count):
        cos, sin = tw_ref[0, l : l + 1, :], tw_ref[1, l : l + 1, :]
        real_part = held[0, pl.ds(l * rows, rows), :]
        imag_part = held[1, pl.ds(l * rows, rows), :]
        held[0, pl.ds(l * rows, rows), :] = real_part * cos - imag_part * sin
        held[1, pl.ds(l * rows, rows), :] = imag_part * cos + real_part * sin
    for h, o_ref in enumerate(o_refs):
        part = slice(h * width, (h + 1) * width)
        for j in range(count):
            real_part = imag_part = None
            for l in range(count):
                cos, sin = root(l * j, count)
                lr = held[0, pl.ds(l * rows, rows), part]
                li = held[1, pl.ds(l * rows, rows), part]
                real_part = add_term(real_part, cos, lr)
                real_part = add_term(real_part, -sin, li)
                imag_part = add_term(imag_part, cos, li)
                imag_part = add_term(imag_part, sin, lr)
            o_ref[j, 0] = real_part
            o_ref[j, 1] = imag_part


def rows_diff(value, before, after):
    count = value.shape[0]
    row = lax.broadcasted_iota(jnp.int32, value.shape, 0)
    low = jnp.where(row == 0, before, pltpu.roll(value, 1, 0))
    high = jnp.where(row == count - 1, after, pltpu.roll(value, count - 1, 0))
    return 0.5 * (high - low)


def cols_diff(value, before, after):
    count = value.shape[1]
    col = lax.broadcasted_iota(jnp.int32, value.shape, 1)
    low = jnp.where(col == 0, before, pltpu.roll(value, 1, 1))
    high = jnp.where(col == count - 1, after, pltpu.roll(value, count - 1, 1))
    return 0.5 * (high - low)


def stress_step(v_ref, prev_ref, next_ref, row_ref, col_ref, w_ref, s_ref, y_ref, n_ref, o_ref):
    layers = v_ref.shape[1]
    i, last = pl.program_id(0), pl.num_programs(0) - 1
    n_ref[...] = v_ref[...]
    for z in range(layers):
        dx, dy, dz = [], [], []
        for c in range(3):
            before = jnp.where(i == 0, row_ref[0, c, z, 7:8, :], prev_ref[c, z, 7:8, :])
            after = jnp.where(i == last, row_ref[1, c, z, 0:1, :], next_ref[c, z, 0:1, :])
            k = c * layers + z
            dx.append(rows_diff(v_ref[c, z], before, after))
            dy.append(
                cols_diff(v_ref[c, z], col_ref[0, :, k : k + 1], col_ref[1, :, k : k + 1])
            )
            low = w_ref[c] if z == 0 else v_ref[c, z - 1]
            if z + 1 < layers:
                dz.append(0.5 * (v_ref[c, z + 1] - low))
            else:
                dz.append(-0.5 * low)
        dilation = dx[0] + dy[1] + dz[2]
        xx = s_ref[0, z] + COURANT * (dilation + 2.0 * dx[0])
        yy = s_ref[1, z] + COURANT * (dilation + 2.0 * dy[1])
        zz = s_ref[2, z] + COURANT * (dilation + 2.0 * dz[2])
        xy = s_ref[3, z] + COURANT * (dy[0] + dx[1])
        xz = s_ref[4, z] + COURANT * (dz[0] + dx[2])
        yz = s_ref[5, z] + COURANT * (dz[1] + dy[2])
        pressure = (xx + yy + zz) / 3.0
        xx, yy, zz = xx - pressure, yy - pressure, zz - pressure
        shear = jnp.sqrt(0.5 * (xx * xx + yy * yy + zz * zz) + (xy * xy + xz * xz + yz * yz))
        limit = y_ref[z] + FRICTION * jnp.maximum(-pressure, 0.0)
        factor = limit / jnp.maximum(shear, limit)
        o_ref[0, z] = pressure + factor * xx
        o_ref[1, z] = pressure + factor * yy
        o_ref[2, z] = pressure + factor * zz
        o_ref[3, z] = factor * xy
        o_ref[4, z] = factor * xz
        o_ref[5, z] = factor * yz


def whole_block(shape):
    return pl.BlockSpec(shape, lambda *_: (0,) * len(shape))


def struct(shape):
    return jax.ShapeDtypeStruct(shape, F32)


def cost(flops, *arrays):
    moved = sum(math.prod(a.shape) * a.dtype.itemsize for a in arrays)
    return pl.CostEstimate(flops=int(flops), bytes_accessed=int(moved), transcendentals=0)


def fault_kernel(
    scale,
    face_ref,
    turns_ref,
    strike_source,
    dip_tw_ref,
    dip_source,
    kernel_ref,
    history_ref,
    velocity_ref,
    stress_ref,
    v_ref,
    row_ref,
    col_ref,
    x1,
    b1,
    b2,
    t1,
    t2,
    u1,
    u2,
    w2,
    held,
    held_part,
    weight,
    strike_tw_ref,
    strike_table_ref,
    dip_table_ref,
    lags,
    lag_held,
    past_ref,
    lag_sem,
    past_sem,
    send_sem,
    recv_sem,
    mirror_sem,
    o_ref,
    v_held,
    stress_held,
    edge_held,
    row_in,
    col_out,
    col_in,
    col_new,
    top_out,
    top_in,
    slab_sem,
    tile_sem,
    edge_sem,
    edge_recv,
):
    count, narrow = x1.shape[0], x1.shape[-1]
    w1, y1, now_ref = b1, x1, lags.at[0]
    parts = count // past_ref.shape[0]
    sizes = {"bx": lax.axis_size("bx"), "by": lax.axis_size("by")}
    place = {"bx": lax.axis_index("bx"), "by": lax.axis_index("by")}

    def device(axis, target):
        if axis == "bx":
            return (target, place["by"])
        return (place["bx"], target)

    strike, dip = place["bx"], place["by"]
    modes, zone = t2.shape[3], min(8, t2.shape[3])

    def active(target):
        return lax.rem(strike + target, 2) == 0

    full = active(dip)
    thin = jnp.logical_and(jnp.logical_not(full), strike == 0)
    forward = jnp.logical_or(full, strike == 0)
    mirror = (lax.rem(sizes["bx"] - strike, sizes["bx"]), sizes["by"] - 1 - dip)

    layers, cells, width = v_held.shape[1:]
    components = past_ref.shape[0]
    lag_loads = [
        pltpu.make_async_copy(
            kernel_ref.at[:, :, 0, l, :], lags.at[:, pl.ds(l * modes, modes), :], lag_sem.at[l]
        )
        for l in range(sizes["by"])
    ]

    def past_loads(i):
        slot = lax.rem(i, 2)
        return [
            pltpu.make_async_copy(
                history_ref.at[:, slot, lax.div(i, 2), :, 0, l, :],
                lag_held.at[slot, :, pl.ds(l * modes, modes), :],
                past_sem.at[slot, l],
            )
            for l in range(sizes["by"])
        ]

    table_loads = [
        pltpu.make_async_copy(source, landing, lag_sem.at[sizes["by"] + i])
        for i, (source, landing) in enumerate(
            ((strike_source, strike_table_ref), (dip_source, dip_table_ref))
        )
    ]
    for load in lag_loads + table_loads:
        load.start()
    barrier = pltpu.get_barrier_semaphore()
    pl.semaphore_signal(barrier, 1, device_id=mirror, device_id_type=pl.DeviceIdType.MESH)
    for axis in ("bx", "by"):

        @pl.loop(1, sizes[axis])
        def _(k):
            target = lax.rem(place[axis] + k, sizes[axis])
            pl.semaphore_signal(
                barrier, 1, device_id=device(axis, target), device_id_type=pl.DeviceIdType.MESH
            )

    pl.semaphore_wait(barrier, sizes["bx"] + sizes["by"] - 1)

    swap = pltpu.make_async_remote_copy(
        src_ref=weight,
        dst_ref=weight,
        send_sem=mirror_sem.at[0],
        recv_sem=mirror_sem.at[1],
        device_id=mirror,
        device_id_type=pl.DeviceIdType.MESH,
    )


    def piece(ref, g, slot):
        if len(ref.shape) == 4 and ref.shape[0] != count:
            return ref.at[g // parts, slot, :, pl.ds(pl.multiple_of(g % parts * narrow, narrow), narrow)]
        if ref is face_ref or ref is o_ref:
            return ref.at[g, slot, :, pl.ds(0, narrow)]
        return ref.at[g, slot]

    def several(ref, g, number):
        if len(ref.shape) == 4 and ref.shape[0] != count:
            lanes = pl.ds(pl.multiple_of(g % parts * narrow, narrow), narrow)
            return ref.at[g // parts, pl.ds(0, number), :, lanes]
        return ref.at[g, pl.ds(0, number)]

    def settle(ref, sem):
        pltpu.make_async_copy(ref, ref, sem).wait()

    def copy(stage, axis, c, k, source, landing):
        me = place[axis]
        target = lax.rem(me + k, sizes[axis])
        return pltpu.make_async_remote_copy(
            src_ref=piece(source, c, target),
            dst_ref=piece(landing, c, me),
            send_sem=send_sem.at[stage, c],
            recv_sem=recv_sem.at[stage, c],
            device_id=device(axis, target),
            device_id_type=pl.DeviceIdType.MESH,
        )

    def own(stage, axis, c, source, landing):
        me = place[axis]
        return pltpu.make_async_copy(
            piece(source, c, me), piece(landing, c, me), recv_sem.at[stage, c]
        )

    def send(stage, axis, c, source, landing):
        @pl.loop(1, sizes[axis])
        def _(k):
            copy(stage, axis, c, k, source, landing).start()

        own(stage, axis, c, source, landing).start()

    def receive(stage, axis, c, source, landing):
        settle(several(landing, c, sizes[axis]), recv_sem.at[stage, c])
        settle(several(landing, c, sizes[axis] - 1), send_sem.at[stage, c])

    def tile(ref, g, slot):
        return ref.at[g, slot, :, pl.ds(0, zone), :]

    def lean(g, k):
        target = lax.rem(dip + k, sizes["by"])
        return pltpu.make_async_remote_copy(
            src_ref=tile(t1, g, target),
            dst_ref=tile(t2, g, dip),
            send_sem=send_sem.at[6, g],
            recv_sem=recv_sem.at[2, g],
            device_id=device("by", target),
            device_id_type=pl.DeviceIdType.MESH,
        )

    def lean_own(g):
        return pltpu.make_async_copy(tile(t1, g, dip), tile(t2, g, dip), recv_sem.at[2, g])

    def spread(g):
        @pl.loop(1, sizes["by"])
        def _(k):
            wanted = active(lax.rem(dip + k, sizes["by"]))

            @pl.when(wanted)
            def _():
                copy(2, "by", g, k, t1, t2).start()

            @pl.when(jnp.logical_and(jnp.logical_not(wanted), strike == 0))
            def _():
                lean(g, k).start()

        @pl.when(full)
        def _():
            own(2, "by", g, t1, t2).start()

        @pl.when(thin)
        def _():
            lean_own(g).start()

    half = sizes["by"] // 2

    def spread_end(g):
        def wait(condition, number, zoned):
            @pl.when(condition)
            def _():
                if zoned:
                    settle(t1.at[g, pl.ds(0, number), :, pl.ds(0, zone), :], send_sem.at[6, g])
                else:
                    settle(t1.at[g, pl.ds(0, number)], send_sem.at[2, g])

        wait(full, half - 1, False)
        wait(jnp.logical_not(full), half, False)
        wait(jnp.logical_and(full, strike == 0), half, True)
        wait(thin, half - 1, True)

    def gather(g):
        @pl.when(full)
        def _():
            settle(t2.at[g], recv_sem.at[2, g])

        @pl.when(thin)
        def _():
            settle(t2.at[g, :, :, pl.ds(0, zone), :], recv_sem.at[2, g])

    stages = (
        ("bx", face_ref, x1),
        ("bx", b1, b2),
        ("by", t1, t2),
        ("by", u1, u2),
        ("bx", w1, w2),
        ("bx", y1, o_ref),
    )

    def go(stage, g):
        axis, source, landing = stages[stage]
        send(stage, axis, g, source, landing)

    def take(stage, g):
        axis, source, landing = stages[stage]
        receive(stage, axis, g, source, landing)

    def enter(g):
        take(0, g)
        strike_forward(sizes["bx"], x1.at[g], b1.at[g])
        go(1, g)

    def across(g):
        take(1, g)
        strike_cells_dft(-1.0, b2.at[g], strike_tw_ref, strike_table_ref, t1.at[g], held_part)
        spread(g)

    def back(g):
        take(3, g)
        strike_cells_dft(1.0, u2.at[g], strike_tw_ref, strike_table_ref, w1.at[g], held_part)
        go(4, g)

    def leave(g):
        take(4, g)
        strike_inverse(sizes["bx"], scale, w2.at[g], y1.at[g])
        go(5, g)

    def remember(i):
        for load in past_loads(i):
            load.wait()
        slot = lax.rem(i, 2)

        @pl.loop(0, cells // 8)
        def _(k):
            rows = pl.ds(pl.multiple_of(k * 8, 8), 8)
            total = lags[1, rows, :] * lag_held[slot, 0, rows, :]
            for h in range(1, lag_held.shape[1]):
                total = total + lags[h + 1, rows, :] * lag_held[slot, h, rows, :]
            past_ref[lax.div(i, 2), slot, rows, :] = total

        @pl.when(i + 2 < 2 * components)
        def _():
            for load in past_loads(i + 2):
                load.start()

    def pick(rows, columns, total, wrap):
        at = lax.broadcasted_iota(jnp.int32, (rows, columns), 0)
        at = at + lax.broadcasted_iota(jnp.int32, (rows, columns), 1)
        at = jnp.where(at == total, 1.0, jnp.where(at == wrap, 1.0, 0.0))
        return at.astype(BF16)

    def place_all(value, table, left):
        total = None
        for _ in range(3):
            piece = value.astype(BF16)
            value = value - piece.astype(F32)
            a, b = (table, piece) if left else (piece, table)
            term = lax.dot_general(a, b, (((1,), (0,)), ((), ())), preferred_element_type=F32)
            total = term if total is None else total + term
        return total

    def mirrored():
        flip = pick(modes, modes, jnp.where(strike == 0, modes, modes - 1), -1)
        for l in range(sizes["by"]):
            other = (sizes["by"] - l) % sizes["by"]
            table = pick(width, width, width if l == 0 else width - 1, 0 if l == 0 else -1)
            value = place_all(now_ref[pl.ds(l * modes, modes), :], table, False)
            weight[pl.ds(other * modes, modes), :] = place_all(value, flip, True)

    def weigh():
        @pl.when(full)
        def _():
            swap.wait_recv()
            weight[...] = scale * (now_ref[...] + weight[...])

        @pl.when(thin)
        def _():
            swap.wait_send()
            if zone < modes:

                @pl.loop(0, count)
                def _(g):
                    t2[g, :, :, pl.ds(zone, modes - zone), :] = jnp.zeros(
                        (*t2.shape[1:3], modes - zone, narrow), F32
                    )

            row = lax.broadcasted_iota(jnp.int32, now_ref.shape, 0)
            weight[...] = jnp.where(lax.rem(row, modes) == 0, scale * now_ref[...], 0.0)

    def respond(c):
        @pl.when(forward)
        def _():
            for h in range(parts):
                gather(c * parts + h)
            dip_forward(
                [t2.at[c * parts + h] for h in range(parts)],
                dip_tw_ref,
                dip_table_ref,
                weight,
                past_ref.at[c],
                held,
            )

        @pl.when(jnp.logical_not(forward))
        def _():
            held[...] = past_ref[c]

        dip_inverse(
            held,
            dip_tw_ref,
            dip_table_ref,
            [u1.at[c * parts + h] for h in range(parts)],
        )
        for h in range(parts):
            go(3, c * parts + h)

    for load in past_loads(0) + past_loads(1):
        load.start()
    size = stress_held.shape[3] - 16
    tiles = cells // size
    block = col_out.shape[2]
    sources = ((0, 3, 4), (3, 1, 5), (4, 5, 2))
    up = {axis: lax.rem(place[axis] + 1, sizes[axis]) for axis in sizes}
    down = {axis: lax.rem(place[axis] + sizes[axis] - 1, sizes[axis]) for axis in sizes}

    def pair(axis, first, last, low, high, slot):
        return [
            pltpu.make_async_remote_copy(
                src_ref=source,
                dst_ref=landing,
                send_sem=edge_sem.at[slot + i],
                recv_sem=edge_recv.at[slot + i],
                device_id=device(axis, target[axis]),
                device_id_type=pl.DeviceIdType.MESH,
            )
            for i, (source, landing, target) in enumerate(((last, low, up), (first, high, down)))
        ]

    stress_rows = []
    for k, c in enumerate(sources[0]):
        stress_rows += pair(
            "bx",
            stress_ref.at[c, :, pl.ds(0, 8), :],
            stress_ref.at[c, :, pl.ds(cells - 8, 8), :],
            row_in.at[0, k],
            row_in.at[1, k],
            2 * k,
        )
    stress_cols = pair("by", col_out.at[0], col_out.at[1], col_in.at[0], col_in.at[1], 6)
    deep = pl.ds(1, layers - 1)
    deep_rows, top_rows = [
        pair(
            "bx",
            v_held.at[:, z, pl.ds(0, 8), :],
            v_held.at[:, z, pl.ds(cells - 8, 8), :],
            row_ref.at[0, :, z],
            row_ref.at[1, :, z],
            slot,
        )
        for z, slot in ((deep, 8), (0, 12))
    ]
    top_cols = pair("by", top_out.at[0], top_out.at[1], top_in.at[0], top_in.at[1], 14)
    new_cols = pair("by", col_new.at[0], col_new.at[1], col_ref.at[0], col_ref.at[1], 10)
    sides = (pl.ds(0, block), pl.ds(width - block, block))
    edge_loads = [
        pltpu.make_async_copy(
            stress_ref.at[c, :, :, side], edge_held.at[i, k], slab_sem.at[3 * i + k]
        )
        for i, side in enumerate(sides)
        for k, c in enumerate(sources[1])
    ]
    velocity_load = pltpu.make_async_copy(velocity_ref, v_held, slab_sem.at[6])
    deep_store = pltpu.make_async_copy(v_held.at[:, deep], v_ref.at[:, deep], slab_sem.at[7])
    top_store = pltpu.make_async_copy(v_held.at[:, 0], v_ref.at[:, 0], slab_sem.at[8])

    def tile_loads(t):
        slot = lax.rem(t, 2)
        row = pl.multiple_of(t * size, 8)
        before = pl.multiple_of(jnp.maximum(row - 8, 0), 8)
        after = pl.multiple_of(jnp.minimum(row + size, cells - 8), 8)
        loads = [
            pltpu.make_async_copy(
                stress_ref.at[:, :, pl.ds(row, size), :],
                stress_held.at[slot, :, :, pl.ds(8, size), :],
                tile_sem.at[slot, 0],
            )
        ]
        for k, c in enumerate(sources[0]):
            for i, (source, landing) in enumerate(((before, 0), (after, size + 8))):
                loads.append(
                    pltpu.make_async_copy(
                        stress_ref.at[c, :, pl.ds(source, 8), :],
                        stress_held.at[slot, c, :, pl.ds(landing, 8), :],
                        tile_sem.at[slot, 1 + 2 * k + i],
                    )
                )
        return loads

    def edges():
        for load in edge_loads:
            load.wait()
        for k in range(3):
            for z in range(layers):
                lane = pl.ds(k * layers + z, 1)
                col_out[0, :, lane] = edge_held[0, k, z, :, 0:1]
                col_out[1, :, lane] = edge_held[1, k, z, :, block - 1 : block]
        for c in stress_cols:
            c.start()

    def slab(t):
        @pl.when(t == 0)
        def _():
            velocity_load.wait()
            for c in stress_rows + stress_cols:
                c.wait_recv()

        @pl.when(t + 1 < tiles)
        def _():
            for load in tile_loads(t + 1):
                load.start()

        for load in tile_loads(t):
            load.wait()
        slot = lax.rem(t, 2)
        rows = pl.ds(pl.multiple_of(t * size, 8), size)
        for component, (sx, sy, sz) in enumerate(sources):
            for z in range(layers):
                k = component * layers + z
                before = jnp.where(t == 0, row_in[0, component, z, 7:8, :], stress_held[slot, sx, z, 7:8, :])
                after = jnp.where(
                    t == tiles - 1,
                    row_in[1, component, z, 0:1, :],
                    stress_held[slot, sx, z, size + 8 : size + 9, :],
                )
                total = rows_diff(stress_held[slot, sx, z, 8 : size + 8, :], before, after)
                total = total + cols_diff(
                    stress_held[slot, sy, z, 8 : size + 8, :],
                    col_in[0, rows, k : k + 1],
                    col_in[1, rows, k : k + 1],
                )
                if z + 1 < layers:
                    total = total + 0.5 * stress_held[slot, sz, z + 1, 8 : size + 8, :]
                if z > 0:
                    total = total - 0.5 * stress_held[slot, sz, z - 1, 8 : size + 8, :]
                value = v_held[component, z, rows, :] + COURANT * total
                v_held[component, z, rows, :] = value
                if z > 0:
                    col_new[0, rows, k : k + 1] = value[:, 0:1]
                    col_new[1, rows, k : k + 1] = value[:, width - 1 : width]

        @pl.when(t == tiles - 1)
        def _():
            deep_store.start()
            for c in deep_rows + new_cols:
                c.start()

    go(0, 0)
    go(0, 1)
    for load in edge_loads:
        load.start()
    for c in stress_rows:
        c.start()
    velocity_load.start()
    for load in tile_loads(0):
        load.start()
    turns = turns_ref[strike]
    strike_tw_ref[...] = jnp.concatenate([turns, jnp.zeros((block - 8, cells), F32)], axis=0).T
    first_tile = 3
    first_back = count + 1
    gap = first_back + parts

    def turn_of(s):
        last, none = components - 1, components
        whole = lax.rem(s + parts - 1, parts) == 0
        step = lax.div(s - 1, parts)
        now = jnp.where(jnp.logical_and(whole, step >= 2), step - 2, none)
        now = jnp.where(now >= last, none, now)
        now = jnp.where(s == gap, last, now)
        early = jnp.where(s == 0, 0, none)
        early = jnp.where(s == first_back + 1, 1, early)
        early = jnp.where(s == gap + 1, 2, early)
        return jnp.where(forward, now, early)

    @pl.loop(0, first_back + count + 2)
    def _(s):
        @pl.when(s < count)
        def _():
            enter(s)

        @pl.when(s + 2 < count)
        def _():
            go(0, s + 2)

        @pl.when(jnp.logical_and(forward, s == 2 * parts + 1))
        def _():
            weigh()

        @pl.when(s == 0)
        def _():
            edges()

        @pl.when(s == 0)
        def _():
            for load in lag_loads + table_loads:
                load.wait()

        @pl.when(jnp.logical_and(s == 0, jnp.logical_not(full)))
        def _():
            mirrored()
            swap.start()

        @pl.when(s < components)
        def _():
            remember(2 * s)
            remember(2 * s + 1)

        turn = turn_of(s)

        @pl.when(turn < components)
        def _():
            respond(turn)

        @pl.when(jnp.logical_and(s > 0, s <= count))
        def _():
            across(s - 1)

        turned = s - first_back - (s > gap).astype(jnp.int32)

        @pl.when(jnp.logical_and(jnp.logical_and(turned >= 0, turned < count), s != gap))
        def _():
            back(turned)

        done = s - first_back - 1 - (s > gap + 1).astype(jnp.int32)

        @pl.when(jnp.logical_and(jnp.logical_and(done >= 0, done < count), s != gap + 1))
        def _():
            leave(done)

        @pl.when(jnp.logical_and(s >= first_tile, s < tiles + first_tile))
        def _():
            slab(s - first_tile)

    @pl.when(jnp.logical_not(forward))
    def _():
        swap.wait_send()

    @pl.loop(0, count)
    def _(g):
        take(5, g)
        spread_end(g)
        c = lax.div(g, parts)
        lanes = pl.ds(pl.multiple_of(lax.rem(g, parts) * narrow, narrow), narrow)
        high = cells // sizes["bx"]
        for b in range(sizes["bx"]):
            rows = pl.ds(b * high, high)
            v_held[c, 0, rows, lanes] = v_held[c, 0, rows, lanes] - (0.5 * COURANT) * o_ref[c, b, :, lanes]

    for c in top_rows:
        c.start()
    top_store.start()
    lane = lax.broadcasted_iota(jnp.int32, (cells, block), 1)
    for i, side in enumerate((0, width - block)):
        at = block - 1 if i else 0
        total = jnp.zeros((cells, block), F32)
        for c in range(components):
            value = v_held[c, 0, :, side : side + block][:, at : at + 1]
            total = jnp.where(lane == c, value, total)
        top_out[i] = total.T[:8]
    for c in top_cols:
        c.start()
    for c in new_cols + deep_rows + top_cols:
        c.wait_recv()
    for i in range(2):
        filled = jnp.concatenate([top_in[i], jnp.zeros((block - 8, cells), F32)], axis=0).T
        for c in range(components):
            col_ref[i, :, c * layers : c * layers + 1] = filled[:, c : c + 1]
    deep_store.wait()
    top_store.wait()
    for c in stress_rows + stress_cols + new_cols + deep_rows + top_cols:
        c.wait_send()
    for c in top_rows:
        c.wait()


def fault_velocity(interface, kernel, history, tables, velocity, stress, scale):
    strike_count, dip_count = lax.axis_size("bx"), lax.axis_size("by")
    count, cells, width = interface.shape
    rows, modes = cells // strike_count, cells // dip_count
    parts = 2 if width % 256 == 0 else 1
    narrow = width // parts
    face = interface.reshape(count, strike_count, rows, width)
    chunks = count * parts
    flat = (chunks, strike_count, rows, narrow)
    wide = (chunks, strike_count, 2, rows, narrow)
    tall = (chunks, dip_count, 2, modes, narrow)
    layers = velocity.shape[1]
    tile, block = min(32, cells), min(128, width)
    operands = (face, *tables, kernel, history, velocity, stress)
    vmem, anywhere = pl.BlockSpec(memory_space=pltpu.VMEM), pl.BlockSpec(memory_space=pl.ANY)
    return pl.pallas_call(
        partial(fault_kernel, scale),
        out_shape=[
            struct(velocity.shape),
            struct((2, count, layers, 8, width)),
            struct((2, cells, block)),
        ],
        in_specs=[anywhere, vmem, anywhere, vmem] + [anywhere] * 5,
        out_specs=[anywhere, vmem, vmem],
        scratch_shapes=[
            *[pltpu.VMEM(s, F32) for s in (flat, wide, wide, tall, tall, tall, tall, wide)],
            pltpu.VMEM((2, cells, width), F32),
            pltpu.VMEM((2, cells, narrow), F32),
            pltpu.VMEM((cells, width), F32),
            pltpu.VMEM((cells, block), F32),
            pltpu.VMEM(tables[1].shape, BF16),
            pltpu.VMEM(tables[3].shape, BF16),
            pltpu.VMEM((kernel.shape[0], cells, width), F32),
            pltpu.VMEM((2, history.shape[0], cells, width), F32),
            pltpu.VMEM((count, 2, cells, width), F32),
            pltpu.SemaphoreType.DMA((dip_count + 2,)),
            pltpu.SemaphoreType.DMA((2, dip_count)),
            pltpu.SemaphoreType.DMA((7, chunks)),
            pltpu.SemaphoreType.DMA((6, chunks)),
            pltpu.SemaphoreType.DMA((2,)),
            pltpu.VMEM(face.shape, F32),
            pltpu.VMEM(velocity.shape, F32),
            pltpu.VMEM((2, 6, layers, tile + 16, width), F32),
            pltpu.VMEM((2, 3, layers, cells, block), F32),
            pltpu.VMEM((2, 3, layers, 8, width), F32),
            pltpu.VMEM((2, cells, block), F32),
            pltpu.VMEM((2, cells, block), F32),
            pltpu.VMEM((2, cells, block), F32),
            pltpu.VMEM((2, 8, cells), F32),
            pltpu.VMEM((2, 8, cells), F32),
            pltpu.SemaphoreType.DMA((9,)),
            pltpu.SemaphoreType.DMA((2, 7)),
            pltpu.SemaphoreType.DMA((16,)),
            pltpu.SemaphoreType.DMA((16,)),
        ],
        compiler_params=pltpu.CompilerParams(
            collective_id=0, has_side_effects=True, vmem_limit_bytes=63 * 1024 * 1024
        ),
        name="fault_velocity",
    )(*operands)


def tile_spec(shape, tile):
    block = shape[:-2] + (tile, shape[-1])
    lead = (0,) * (len(shape) - 2)
    return pl.BlockSpec(block, lambda i: lead + (i, 0))


def halo_specs(shape, tile):
    block = shape[:-2] + (8, shape[-1])
    lead = (0,) * (len(shape) - 2)
    step, last = tile // 8, shape[-2] // 8 - 1
    return [
        pl.BlockSpec(block, lambda i: lead + (jnp.maximum(i * step - 1, 0), 0)),
        pl.BlockSpec(block, lambda i: lead + (jnp.minimum((i + 1) * step, last), 0)),
    ]


def local(interface_velocity, history, kernel, velocity, stress, cohesion):
    strike_count, dip_count = lax.axis_size("bx"), lax.axis_size("by")
    _, layers, cells, width = velocity.shape
    strike_length, dip_length = cells * strike_count, width * dip_count
    scale = 1.0 / math.sqrt(strike_length * dip_length)
    turn = np.outer(np.arange(strike_count), np.arange(cells)) * (2.0 * math.pi / strike_length)
    turns = np.zeros((strike_count, 8, cells), np.float32)
    turns[:, 0], turns[:, 1] = np.cos(turn), np.sin(turn)
    lane = np.outer(np.arange(dip_count), np.arange(width)) * (2.0 * math.pi / dip_length)
    dip_tw = jnp.asarray(np.stack([np.cos(lane), np.sin(lane)]).astype(np.float32))
    dip_table = square_table(width)
    strike_table = square_table(cells)
    tables = (jnp.asarray(turns), strike_table, dip_tw, dip_table)

    velocity_part, rows, cols = fault_velocity(
        interface_velocity, kernel, history, tables, velocity, stress, scale
    )
    tile = min(64, cells)
    return pl.pallas_call(
        stress_step,
        grid=(cells // tile,),
        in_specs=[
            tile_spec(velocity.shape, tile),
            *halo_specs(velocity.shape, tile),
            whole_block(rows.shape),
            tile_spec(cols.shape, tile),
            tile_spec(interface_velocity.shape, tile),
            tile_spec(stress.shape, tile),
            tile_spec(cohesion.shape, tile),
        ],
        out_specs=[tile_spec(velocity.shape, tile), tile_spec(stress.shape, tile)],
        out_shape=[struct(velocity.shape), struct(stress.shape)],
        cost_estimate=cost(2e7, stress, stress, velocity),
        name="stress_step",
    )(velocity_part, velocity_part, velocity_part, rows, cols, interface_velocity, stress, cohesion)


def solution(mesh):
    return jax.shard_map(
        local,
        mesh=mesh,
        in_specs=(
            P(None, "bx", "by"),
            P(None, None, None, "by", "bx", None, None),
            P(None, "by", "bx", None, None),
            P(None, None, "bx", "by"),
            P(None, None, "bx", "by"),
            P(None, "bx", "by"),
        ),
        out_specs=(P(None, None, "bx", "by"), P(None, None, "bx", "by")),
        check_vma=False,
    )
```
